32 devices in a mesh: blocks: 8 (over y, x, core), slab: 4 (over z).
Axes of the slice: x: 2, y: 2, z: 4, core: 2. Of those that a mesh axis runs over, the one named last changes fastest.
Arguments:
- populations: float32 [19, 4, 8, 4096], P(None, 'slab', 'blocks'), may hold values from -6 to 6
- w_in: bfloat16 [512, 19], replicated, may hold values from -1.25 to 1.25
- w_mid: bfloat16 [1, 512, 512], replicated, may hold values from -0.25 to 0.25
- w_out: bfloat16 [19, 512], replicated, may hold values from -0.25 to 0.25
- cotangent: float32 [19, 4, 8, 4096], P(None, 'slab', 'blocks'), may hold values from -6 to 6
- face_source: int32 [8, 4], replicated, may hold values from 0 to 7, as said below
- face_level: int32 [4, 8, 6], P('slab', 'blocks'), may hold values 0 or 1
- face_quadrant: int32 [4, 8, 6], P('slab', 'blocks'), may hold values from 0 to 3
Outputs:
- final: float32 [19, 4, 8, 4096], P(None, 'slab', 'blocks')
- grad_pops: float32 [19, 4, 8, 4096], P(None, 'slab', 'blocks')
- grad_in: float32 [512, 19], replicated
- grad_mid: float32 [1, 512, 512], replicated
- grad_out: float32 [19, 512], replicated
The draws below stay inside these ranges and needn't reach their ends.
Inputs may be any that keep to these rules, and one draw needn't show every extreme that they name: face_source is symmetric: face_source[face_source[b, f], f xor 1] = b. The +y and -y neighbours of block b are the same block, b xor 1. Every neighbour's index differs from the block's by at most 3 modulo 8, never by 0, and that distance is reached.
All inputs are finite; a program needn't handle non-finite values. No bound on the sum of `face_level` on one device may be relied on, other than what follows from the above.
Results may differ from the reference program's by a relative error of at most 0.0088.
Values sent between devices are 32-bit elements; how exact they have to be, the bound alone decides.
A program may use at most 128 MiB of HBM per device.

```python
from functools import partial
import jax
import jax.numpy as jnp
from jax import lax

Q = 19
HID = 512
MIDS = 1
S = 16
STEPS = 2
CELLS = 4096
GX = 4
CELLS_ALL = 131072
N_BLOCKS = 8
N_SLAB = 4


def placement_tables(key):
    flips = jax.random.randint(jax.random.fold_in(key, 7), (GX,), 0, 2).astype(jnp.int32)
    anchor = jax.random.randint(jax.random.fold_in(key, 11), (), 0, GX).astype(jnp.int32)
    mirror = jax.random.randint(jax.random.fold_in(key, 13), (), 0, 2).astype(jnp.int32)
    follow = (anchor + 1) % GX
    flips = flips.at[follow].set(1 - flips[anchor])
    location = jnp.arange(GX * 2, dtype=jnp.int32)
    column = location // 2
    stored = location % 2
    parity = jnp.bitwise_xor(stored, flips[column])
    next_column = (column + 1) % GX
    prior_column = (column + GX - 1) % GX
    forward_x = next_column * 2 + jnp.bitwise_xor(parity, flips[next_column])
    backward_x = prior_column * 2 + jnp.bitwise_xor(parity, flips[prior_column])
    plus_x = jnp.where(mirror == 1, backward_x, forward_x)
    minus_x = jnp.where(mirror == 1, forward_x, backward_x)
    other_y = column * 2 + (1 - stored)
    return jnp.stack([plus_x, minus_x, other_y, other_y], axis=1).astype(jnp.int32)


def draw_face_source(key, part):
    return placement_tables(key)


def with_ends(array, key, low, high):
    spot = [jax.random.randint(jax.random.fold_in(key, axis), (), 0, length) for axis, length in enumerate(array.shape)]
    longest = array.shape.index(max(array.shape))
    beside = spot[:longest] + [(spot[longest] + 1) % array.shape[longest]] + spot[longest + 1:]
    return array.at[tuple(spot)].set(low).at[tuple(beside)].set(high)


def level_of(stream_key, dims, shards, low, high):
    def one(dim, shards_of):
        heights = jax.random.uniform(jax.random.fold_in(jax.random.fold_in(stream_key, 6), dim), (shards_of,), jnp.float32, low / len(shards), high / len(shards))
        return jnp.repeat(jnp.exp(heights), dims[dim] // shards_of).reshape((-1,) + (1,) * (len(dims) - dim - 1))

    level = one(*shards[0])
    for cut in shards[1:]:
        level = level * one(*cut)
    return level


def centred(rng, extent, spread, most, split=(), kind=jnp.bfloat16):
    drawn = jax.random.normal(rng, extent, jnp.float32) * spread
    if len(split) > 0:
        drawn = level_of(rng, extent, split, -0.22, 0.18) * drawn
    return jnp.clip(drawn, min=-most, max=most).astype(kind)


def setup_inputs(seed: int = 0) -> dict:
    key_list = jax.random.split(jax.random.key(seed), 9)
    populations = centred(key_list[0], (Q, N_SLAB, N_BLOCKS, CELLS), 1.0, 6.0, ((1, 4), (2, 8)), jnp.float32)
    w_in = centred(key_list[1], (HID, Q), Q ** -0.5, 1.25)
    w_mid = centred(key_list[2], (MIDS, HID, HID), HID ** -0.5, 0.25)
    w_out = centred(key_list[3], (Q, HID), HID ** -0.5, 0.25)
    cotangent = centred(key_list[4], (Q, N_SLAB, N_BLOCKS, CELLS), 1.0, 6.0, ((1, 4), (2, 8)), jnp.float32)
    face_source = draw_face_source(jax.random.fold_in(key_list[8], 71), 0)
    face_level = with_ends((jax.random.randint(key_list[6], (N_SLAB, N_BLOCKS, 6), 0, 2) < 1).astype(jnp.int32), jax.random.fold_in(key_list[6], 1), 0, 1)
    face_quadrant = with_ends(jax.random.randint(key_list[7], (N_SLAB, N_BLOCKS, 6), 0, 4), jax.random.fold_in(key_list[7], 1), 0, 3).astype(jnp.int32)
    return {"populations": populations, "w_in": w_in, "w_mid": w_mid, "w_out": w_out, "cotangent": cotangent, "face_source": face_source, "face_level": face_level, "face_quadrant": face_quadrant}


VELOCITIES = [(0, 0, 0), (1, 0, 0), (-1, 0, 0), (0, 1, 0), (0, -1, 0), (0, 0, 1), (0, 0, -1), (1, 1, 0), (-1, -1, 0), (1, -1, 0), (-1, 1, 0), (1, 0, 1), (-1, 0, -1), (1, 0, -1), (-1, 0, 1), (0, 1, 1), (0, -1, -1), (0, 1, -1), (0, -1, 1)]
OPPOSITE = [0, 2, 1, 4, 3, 6, 5, 8, 7, 10, 9, 12, 11, 14, 13, 16, 15, 18, 17]

def face_members(face_id):
    along = face_id // 2
    sign_value = 1 if face_id % 2 == 0 else -1
    return [which for which in range(19) if VELOCITIES[which][along] == sign_value]

def face_layers(collided, block_side):
    cube_view = collided.reshape(collided.shape[0], block_side, block_side, block_side)
    sheets = []
    for face_id in range(6):
        along = face_id // 2
        layer_index = block_side - 1 if face_id % 2 == 0 else 0
        members = jnp.stack([cube_view[which] for which in face_members(face_id)])
        layer_sheet = lax.index_in_dim(members, layer_index, along + 1, keepdims=False)
        sheets.append(layer_sheet.reshape(5, block_side * block_side))
    return jnp.stack(sheets)

def refine_sheet(layer_sheet, levels, quadrant, block_side):
    square = layer_sheet.reshape(5, block_side, block_side)
    half_side = block_side // 2
    row_start = (quadrant // 2 * half_side).astype(jnp.int32)
    col_start = (quadrant % 2 * half_side).astype(jnp.int32)
    corner_part = lax.dynamic_slice(square, (jnp.zeros((), jnp.int32), row_start, col_start), (5, half_side, half_side))
    enlarged = jnp.repeat(jnp.repeat(corner_part, 2, axis=1), 2, axis=2)
    return jnp.where(levels == 1, enlarged, square).reshape(5, block_side * block_side)

def stream_block(collided, ghosts, block_side):
    cube_view = collided.reshape(collided.shape[0], block_side, block_side, block_side)
    shape3 = (block_side, block_side, block_side)
    coords = [lax.broadcasted_iota(jnp.int32, shape3, along) for along in range(3)]
    results = []
    for which in range(19):
        vector = VELOCITIES[which]
        shifted = jnp.roll(cube_view[which], shift=vector, axis=(0, 1, 2))
        crossed = jnp.zeros(shape3, jnp.int32)
        ghost_sum = jnp.zeros(shape3, jnp.float32)
        for along in range(3):
            if vector[along] != 0:
                leaving = coords[along] == (0 if vector[along] == 1 else block_side - 1)
                face_id = 2 * along + (0 if vector[along] == -1 else 1)
                position = face_members(face_id ^ 1).index(which)
                others = [other for other in range(3) if other != along]
                square = ghosts[face_id, position].reshape(block_side, block_side)
                square = jnp.roll(square, shift=(vector[others[0]], vector[others[1]]), axis=(0, 1))
                volume = jnp.expand_dims(square, along)
                ghost_sum = ghost_sum + jnp.where(leaving, volume, jnp.float32(0.0))
                crossed = crossed + leaving.astype(jnp.int32)
        chosen = jnp.where(crossed == 0, shifted, jnp.where(crossed == 1, ghost_sum, cube_view[OPPOSITE[which]]))
        results.append(chosen.reshape(-1))
    return jnp.stack(results)

def contract(left, right):
    return lax.dot_general(left, right, (((1,), (1,)), ((), ())), preferred_element_type=jnp.float32)

def squared(hidden):
    wide_value = hidden.astype(jnp.float32)
    return wide_value * wide_value

def collide_forward(state, w_in, w_mid, w_out):
    inputs_bf = state.astype(jnp.bfloat16)
    layers = [jnp.tanh(jnp.dot(w_in, inputs_bf, preferred_element_type=jnp.float32)).astype(jnp.bfloat16)]
    for depth in range(w_mid.shape[0]):
        layers.append(jnp.tanh(jnp.dot(w_mid[depth], layers[-1], preferred_element_type=jnp.float32)).astype(jnp.bfloat16))
    collided = state + jnp.dot(w_out, layers[-1], preferred_element_type=jnp.float32)
    return (collided, inputs_bf, layers)

def collide_backward(collided_bar, inputs_bf, layers, w_in, w_mid, w_out):
    delta_bf = collided_bar.astype(jnp.bfloat16)
    grad_out = contract(delta_bf, layers[-1])
    signal = (jnp.dot(w_out.T, delta_bf, preferred_element_type=jnp.float32) * (1.0 - squared(layers[-1]))).astype(jnp.bfloat16)
    mid_parts = []
    for depth in reversed(range(w_mid.shape[0])):
        mid_parts.insert(0, contract(signal, layers[depth]))
        signal = (jnp.dot(w_mid[depth].T, signal, preferred_element_type=jnp.float32) * (1.0 - squared(layers[depth]))).astype(jnp.bfloat16)
    grad_in = contract(signal, inputs_bf)
    state_bar = collided_bar + jnp.dot(w_in.T, signal, preferred_element_type=jnp.float32)
    return (state_bar, grad_in, jnp.stack(mid_parts), grad_out)

def stream_all(collided, face_source, face_level, face_quadrant):
    outward = jax.vmap(jax.vmap(partial(face_layers, block_side=S)))(collided)
    lateral = [jnp.take(outward[:, :, face_id ^ 1], face_source[:, face_id], axis=1) for face_id in range(4)]
    from_above = jnp.roll(outward[:, :, 5], -1, axis=0)
    from_below = jnp.roll(outward[:, :, 4], 1, axis=0)
    sheets = jnp.stack(lateral + [from_above, from_below], axis=2)
    ghosts = jax.vmap(jax.vmap(jax.vmap(partial(refine_sheet, block_side=S))))(sheets, face_level, face_quadrant)
    return jax.vmap(jax.vmap(partial(stream_block, block_side=S)))(collided, ghosts)

def reference(populations, w_in, w_mid, w_out, cotangent, face_source, face_level, face_quadrant):
    state = jnp.transpose(populations, (1, 2, 0, 3))
    whole_shape = state.shape
    flat_shape = (whole_shape[0] * whole_shape[1], Q, CELLS)
    streamer = partial(stream_all, face_source=face_source, face_level=face_level, face_quadrant=face_quadrant)

    def collide_one(block):
        return collide_forward(block, w_in, w_mid, w_out)[0]

    def pull_one(pair):
        block, upstream = pair
        collided, inputs_bf, layers = collide_forward(block, w_in, w_mid, w_out)
        return collide_backward(upstream, inputs_bf, layers, w_in, w_mid, w_out)
    history = []
    for step_id in range(STEPS):
        history.append(state)
        collided = lax.map(collide_one, state.reshape(flat_shape)).reshape(whole_shape)
        state = streamer(collided)
    final_state = state
    state_bar = jnp.transpose(cotangent, (1, 2, 0, 3))
    total_in = jnp.zeros((HID, Q), jnp.float32)
    total_mid = jnp.zeros((MIDS, HID, HID), jnp.float32)
    total_out = jnp.zeros((Q, HID), jnp.float32)
    for step_id in reversed(range(STEPS)):
        earlier_state = history[step_id]
        collided = lax.map(collide_one, earlier_state.reshape(flat_shape)).reshape(whole_shape)
        unused, stream_pull = jax.vjp(streamer, collided)
        collided_bar, = stream_pull(state_bar)
        flat_bar, part_in, part_mid, part_out = lax.map(pull_one, (earlier_state.reshape(flat_shape), collided_bar.reshape(flat_shape)))
        state_bar = flat_bar.reshape(whole_shape)
        total_in = total_in + lax.optimization_barrier(jnp.sum(part_in, axis=0))
        total_mid = total_mid + lax.optimization_barrier(jnp.sum(part_mid, axis=0))
        total_out = total_out + lax.optimization_barrier(jnp.sum(part_out, axis=0))
    grad_scale = float(CELLS_ALL) ** (-0.5)
    return (jnp.transpose(final_state, (2, 0, 1, 3)), jnp.transpose(state_bar, (2, 0, 1, 3)), total_in * grad_scale, total_mid * grad_scale, total_out * grad_scale)
```

```python
import functools

import jax
import jax.numpy as jnp
from jax import lax
from jax.experimental import pallas as pl
from jax.experimental.pallas import tpu as pltpu
from jax.sharding import PartitionSpec as P

REACH = 3
R = 24
S = 16
A = S * S
LANES = 128
HALVES = A // LANES
CHUNK = 1024
LINES = CHUNK // LANES
BLOCK = S + 2
PITCH = HALVES * BLOCK
ROWS = R * PITCH
MESH = pl.DeviceIdType.MESH
F32, BF16 = jnp.float32, jnp.bfloat16

VELOCITIES = [
    (0, 0, 0),
    (1, 0, 0),
    (-1, 0, 0),
    (0, 1, 0),
    (0, -1, 0),
    (0, 0, 1),
    (0, 0, -1),
    (1, 1, 0),
    (-1, -1, 0),
    (1, -1, 0),
    (-1, 1, 0),
    (1, 0, 1),
    (-1, 0, -1),
    (1, 0, -1),
    (-1, 0, 1),
    (0, 1, 1),
    (0, -1, -1),
    (0, 1, -1),
    (0, -1, 1),
]
Q = len(VELOCITIES)
OPPOSITE = [VELOCITIES.index((-a, -b, -c)) for a, b, c in VELOCITIES]
FACED = 5
SHEET = 2 * HALVES * FACED
SHEET_ROWS = 24


def members(axis, side):
    return [q for q, v in enumerate(VELOCITIES) if v[axis] == (1, -1)[side]]


def place(q, axis):
    side = 0 if VELOCITIES[q][axis] == 1 else 1
    return side, members(axis, side).index(q)


def base(q, half):
    return q * PITCH + half * BLOCK + 1


def load(ref, q, half, off=0):
    return ref[pl.ds(base(q, half) + off, S), :]


def save(ref, q, half, value):
    ref[pl.ds(base(q, half), S), :] = value


def get_lines(ref, i):
    first = i * (LINES // HALVES)
    return jnp.concatenate(
        [ref[pl.ds(j % HALVES * BLOCK + 1 + j // HALVES + first, R, stride=PITCH), :] for j in range(LINES)], axis=1
    )


def put_lines(ref, i, value):
    first = i * (LINES // HALVES)
    for j in range(LINES):
        at = pl.ds(j % HALVES * BLOCK + 1 + j // HALVES + first, R, stride=PITCH)
        ref[at, :] = value[:, j * LANES : (j + 1) * LANES]


def from_cells(dst, src):
    for q in range(Q):
        for half in range(HALVES):
            save(dst, q, half, src[pl.ds(q * S * HALVES + half, S, stride=HALVES), :])


def to_cells(dst, q, half, value):
    dst[pl.ds(q * S * HALVES + half, S, stride=HALVES), :] = value


class Grid:
    def __init__(self):
        self.x = lax.broadcasted_iota(jnp.int32, (S, LANES), 0)
        self.lane = lax.broadcasted_iota(jnp.int32, (S, LANES), 1)
        self.y = self.lane // S
        self.z = self.lane % S
        self.lane1 = lax.broadcasted_iota(jnp.int32, (1, LANES), 1)
        self.y1, self.z1 = self.lane1 // S, self.lane1 % S


def roll(x, shift):
    shift %= LANES
    return x if shift == 0 else pltpu.roll(x, shift, 1)


def fan(x, shift, stride):
    return pltpu.roll(x, shift % LANES, 1, stride=stride, stride_axis=0)


def carry(g, pair, step, lane):
    if step == 1:
        return [pair[0], jnp.where(lane < LANES - S, pair[1], pair[0])]
    if step == -1:
        return [jnp.where(lane >= S, pair[0], pair[1]), pair[1]]
    return pair


def wide(row):
    return jnp.broadcast_to(row, (8, LANES))


def spread_y(row_of, side):
    shift = 0 if side == 0 else -(LANES - S)
    return jnp.concatenate([fan(wide(row_of(half)), shift, S) for half in range(HALVES)], axis=0)


def spread_z(g, row_of, z, dy):
    pair = carry(g, [row_of(half) for half in range(HALVES)], dy, g.lane1)
    return [
        jnp.concatenate([fan(wide(row), z - (S - 1) + S * dy + 8 * part, 1) for part in range(2)], axis=0) for row in pair
    ]


def total_rows(x):
    return jnp.sum(x, axis=0, keepdims=True)


def sheet_row(side, half, r):
    return (side * HALVES + half) * FACED + r


def put_row(ref, side, half, r, value):
    at = sheet_row(side, half, r)
    ref[at : at + 1, :] = value


def fold_y(x, high):
    shift = S if high else 0
    return [total_rows(fan(x[8 * part : 8 * part + 8], shift, S)) for part in range(2)]


def fold_z(x, z):
    return total_rows(sum(fan(x[8 * part : 8 * part + 8], 8 * part - z, 1) for part in range(2)))


def gather_sheets(g, post, sheets):
    for q, v in enumerate(VELOCITIES):
        if v[0]:
            side, r = place(q, 0)
            for half in range(HALVES):
                at = base(q, half) + (S - 1 if v[0] == 1 else 0)
                put_row(sheets.at[0], side, half, r, post[at : at + 1, :])
        if v[1]:
            side, r = place(q, 1)
            high = v[1] == 1
            x = jnp.where(g.y == (7 if high else 0), load(post, q, 1 if high else 0), 0.0)
            for part, row in enumerate(fold_y(x, high)):
                put_row(sheets.at[1], side, part, r, row)
        if v[2]:
            side, r = place(q, 2)
            z = S - 1 if v[2] == 1 else 0
            for half in range(HALVES):
                row = fold_z(jnp.where(g.z == z, load(post, q, half), 0.0), z)
                put_row(sheets.at[2], side, half, r, row)


def inside_z(z, dz):
    return z != (0 if dz == 1 else S - 1)


def gather_bars(g, bar, tmp):
    last = LANES // S - 1
    for q, (dx, dy, dz) in enumerate(VELOCITIES):
        if dx:
            side, r = place(q, 0)
            rows = []
            for half in range(HALVES):
                at = base(q, half) + (0 if dx == 1 else S - 1)
                row = bar[at : at + 1, :]
                rows.append(jnp.where(inside_z(g.z1, dz), row, 0.0) if dz else row)
            rows = [roll(row, -S * dy - dz) for row in carry(g, rows, -dy, g.lane1)]
            if dy:
                half, y = (1, last) if dy == 1 else (0, 0)
                rows[half] = jnp.where(g.y1 == y, 0.0, rows[half])
            for half in range(HALVES):
                put_row(tmp.at[0], side, half, r, rows[half])
        if dy:
            side, r = place(q, 1)
            keep = g.y == (0 if dy == 1 else last)
            if dz:
                keep &= inside_z(g.z, dz)
            if dx:
                keep &= g.x != (S - 1 if dx == 1 else 0)
            x = jnp.where(keep, load(bar, q, 0 if dy == 1 else 1, dx), 0.0)
            for part, row in enumerate(fold_y(x, dy == -1)):
                put_row(tmp.at[1], side, part, r, roll(row, -dz))
        if dz:
            side, r = place(q, 2)
            z = 0 if dz == 1 else S - 1
            rows = []
            for half in range(HALVES):
                keep = g.z == z
                if dx:
                    keep &= g.x != (S - 1 if dx == 1 else 0)
                if dy and half == (0 if dy == 1 else 1):
                    keep &= g.y != (0 if dy == 1 else last)
                rows.append(fold_z(jnp.where(keep, load(bar, q, half, dx), 0.0), z))
            rows = [roll(row, -S * dy) for row in carry(g, rows, -dy, g.lane1)]
            if dy:
                half, y = (1, last) if dy == 1 else (0, 0)
                rows[half] = jnp.where(g.y1 == y, 0.0, rows[half])
            for half in range(HALVES):
                put_row(tmp.at[2], side, half, r, rows[half])


def refined(halves, pick, transposed):
    sheet = jnp.concatenate(halves, axis=1)
    hi = sheet.astype(BF16).astype(F32)
    rest = sheet - hi
    mid = rest.astype(BF16).astype(F32)
    parts = jnp.concatenate([hi, mid, rest - mid], axis=0).astype(BF16)
    dims = (((1,), (1 if transposed else 0,)), ((), ()))
    r = lax.dot_general(parts, pick, dims, preferred_element_type=F32)
    return r[:8] + r[8:16] + r[16:]


def sheet_halves(ref, side):
    return [ref[pl.ds(sheet_row(side, half, 0), 8), :] for half in range(HALVES)]


def send_bars(g, bar, tmp, sheets, picks):
    gather_bars(g, bar, tmp)
    for axis in range(3):
        for side in range(2):
            out = refined(sheet_halves(tmp.at[axis], side), picks[pick_at(axis, side, True)], True)
            for half in range(HALVES):
                sheets[axis, pl.ds(sheet_row(side, half, 0), FACED), :] = out[:FACED, half * LANES : (half + 1) * LANES]


def pick_at(axis, side, back):
    if axis == 0:
        return side
    return 2 + 8 // 2 * back + 2 * (axis - 1) + side


def build_picks(level, quadrant, picks, back, axes):
    lane = lax.broadcasted_iota(jnp.int32, (1, A), 1)
    source = lax.broadcasted_iota(jnp.int32, (A, A), 0)
    half = S // 2

    def turned(axis, i):
        if axis == 0:
            return i
        if axis == 1:
            return i // LANES * LANES + (7 - i // S % 8) * S + i % S
        return i // S * S + (S - 1 - i % S)

    for axis in axes:
        for side in range(2):
            face = 2 * axis + 1 - side
            quad = quadrant[0, 0, face]
            first, second = quad // 2, quad % 2
            if axis == 2:
                first, second = second, first

            def wanted(i):
                fine = (first * half + i // S // 2) * S + second * half + i % S // 2
                return jnp.where(level[0, 0, face] == 1, fine, i)

            want = turned(axis, wanted(lane)) if back else wanted(turned(axis, lane))
            picks[pick_at(axis, side, back)] = jnp.where(source == want, 1.0, 0.0).astype(BF16)


def slot_of(source, blocks, face):
    me = lax.axis_index("blocks")
    distance = lax.rem(source[face, me] - me + blocks, blocks)
    distance = jnp.where(distance > blocks // 2, distance - blocks, distance)
    slot = jnp.where(distance < 0, distance + REACH, distance + REACH - 1)
    return jnp.clip(slot, 0, 2 * REACH - 1)


def ghost_row(axis, side, half, r):
    return (((axis - 1) * 2 + side) * HALVES + half) * 8 + r


def settle(recv, slots, picks, post, ghosts):
    for side in range(2):
        slot = slots[1 - side]
        halves = [recv[slot, pl.ds(sheet_row(side, half, 0), 8), :] for half in range(HALVES)]
        out = refined(halves, picks[pick_at(0, side, False)], False)
        for r, q in enumerate(members(0, side)):
            for half in range(HALVES):
                at = base(q, half) + (-1 if side == 0 else S)
                post[at : at + 1, :] = out[r : r + 1, half * LANES : (half + 1) * LANES]
    for axis in (1, 2):
        for side in range(2):
            slot = 2 * REACH if axis == 1 else 2 * REACH + (2 if side == 0 else 1)
            out = refined(sheet_halves(recv.at[slot], side), picks[pick_at(axis, side, False)], False)
            for half in range(HALVES):
                at = ghost_row(axis, side, half, 0)
                ghosts[at : at + 8, :] = out[:, half * LANES : (half + 1) * LANES]


def stream(g, post, ghosts, shifted, store):
    last = LANES // S - 1
    used = [0]

    def moved(value, dx):
        if not dx:
            return value
        at = used[0] * BLOCK + 1
        used[0] += 1
        shifted[pl.ds(at, S), :] = value
        return shifted[pl.ds(at - dx, S), :]

    for q, (dx, dy, dz) in enumerate(VELOCITIES):
        t = [load(post, q, half, -dx) for half in range(HALVES)]
        if dy:
            side, r = place(q, 1)

            def row_y(half):
                at = ghost_row(1, side, half, r)
                return ghosts[at : at + 1, :]

            halo = moved(spread_y(row_y, side), dx)
            if dy == 1:
                inner = g.lane < LANES - S
                t = [jnp.where(inner, t[0], halo), jnp.where(inner, t[1], t[0])]
            else:
                inner = g.lane >= S
                t = [jnp.where(inner, t[0], t[1]), jnp.where(inner, t[1], halo)]
        t = [roll(x, S * dy + dz) for x in t]
        if dz:
            side, r = place(q, 2)
            z = 0 if dz == 1 else S - 1

            def row_z(half):
                at = ghost_row(2, side, half, r)
                return ghosts[at : at + 1, :]

            halo = [moved(x, dx) for x in spread_z(g, row_z, z, dy)]
            t = [jnp.where(g.z == z, halo[half], t[half]) for half in range(HALVES)]
        for half in range(HALVES):
            two = crossed(g, half, dx, dy, dz)
            if two is not None:
                t[half] = jnp.where(two, load(post, OPPOSITE[q], half), t[half])
            store(q, half, t[half])


def crossed(g, half, dx, dy, dz):
    if (dx != 0) + (dy != 0) + (dz != 0) < 2:
        return None
    if dy and half != (0 if dy == 1 else 1):
        return None
    on = None
    for d, c, top in ((dx, g.x, S - 1), (dy, g.y, LANES // S - 1), (dz, g.z, S - 1)):
        if d:
            hit = c == (0 if d == 1 else top)
            on = hit if on is None else on & hit
    return on


def stream_back(g, bar, recv, slots, store):
    last = LANES // S - 1
    for q, (dx, dy, dz) in enumerate(VELOCITIES):
        t = [load(bar, q, half, dx) for half in range(HALVES)]
        t = [roll(x, -S * dy - dz) for x in carry(g, t, -dy, g.lane)]
        faces = []
        if dx:
            side, r = place(q, 0)
            slot = slots[side]
            rows = [recv[slot, pl.ds(sheet_row(side, half, r), 1), :] for half in range(HALVES)]
            rows = [jnp.broadcast_to(row, (S, LANES)) for row in rows]
            faces.append((rows, [g.x == (S - 1 if dx == 1 else 0)] * 2))
        if dy:
            side, r = place(q, 1)
            full = spread_y(lambda half: recv[2 * REACH, pl.ds(sheet_row(side, half, r), 1), :], side)
            mask = g.y == (last if dy == 1 else 0)
            faces.append(([full, full], [mask if half == (1 if dy == 1 else 0) else None for half in range(HALVES)]))
        if dz:
            side, r = place(q, 2)
            slot = 2 * REACH + (1 if side == 0 else 2)
            z = S - 1 if dz == 1 else 0
            full = spread_z(g, lambda half: recv[slot, pl.ds(sheet_row(side, half, r), 1), :], z, 0)
            faces.append((full, [g.z == z] * 2))
        for half in range(HALVES):
            here = [(value[half], mask[half]) for value, mask in faces if mask[half] is not None]
            out = t[half]
            if len(here) == 1:
                out = jnp.where(here[0][1], here[0][0], out)
            if len(here) == 2:
                (va, ma), (vb, mb) = here
                both = va + vb + load(bar, OPPOSITE[q], half)
                out = jnp.where(mb, jnp.where(ma, both, vb), jnp.where(ma, va, out))
            store(q, half, out)


def mm(a, b):
    return jnp.dot(a, b, preferred_element_type=F32)


def outer(a, b):
    return lax.dot_general(a, b, (((1,), (1,)), ((), ())), preferred_element_type=F32)


def slope(h):
    wide_h = h.astype(F32)
    return 1.0 - wide_h * wide_h


def span(i):
    return pl.ds(pl.multiple_of(i * CHUNK, CHUNK), CHUNK)


def padded_rows(src, tall, flat, flipped):
    tall[...] = jnp.zeros(tall.shape, F32)
    tall[:Q] = src[...].astype(F32)
    flat[...] = tall[...].astype(BF16)
    flipped[...] = tall[...].T.astype(BF16)


OFFSETS = [d for d in range(-REACH, REACH + 1) if d != 0]


class Exchange:
    def __init__(self, blocks, slabs):
        me, level = lax.axis_index("blocks"), lax.axis_index("slab")
        self.side = [lax.rem(me - d + blocks, blocks) for d in OFFSETS]
        self.other = me + 1 - 2 * lax.rem(me, 2)
        self.above, self.below = lax.rem(level + 1, slabs), lax.rem(level + slabs - 1, slabs)

    def greet(self):
        barrier = pltpu.get_barrier_semaphore()
        for target in self.side:
            pl.semaphore_signal(barrier, inc=1, device_id={"blocks": target}, device_id_type=MESH)
        for target in (self.above, self.below):
            pl.semaphore_signal(barrier, inc=1, device_id={"slab": target}, device_id_type=MESH)

    def meet(self):
        pl.semaphore_wait(pltpu.get_barrier_semaphore(), len(self.side) + 2)

    def send(self, sheets, recv, sems):
        plan = [(0, i, {"blocks": target}) for i, target in enumerate(self.side)]
        plan.append((1, 2 * REACH, {"blocks": self.other}))
        plan.append((2, 2 * REACH + 1, {"slab": self.below}))
        plan.append((2, 2 * REACH + 2, {"slab": self.above}))
        copies = []
        for which, slot, device in sorted(plan, key=lambda row: -row[0]):
            copy = pltpu.make_async_remote_copy(
                src_ref=sheets.at[which, pl.ds(0, SHEET)], dst_ref=recv.at[slot, pl.ds(0, SHEET)],
                send_sem=sems.at[0, slot], recv_sem=sems.at[1, slot],
                device_id=device, device_id_type=MESH,
            )
            copy.start()
            copies.append(copy)
        return copies


def arrive(copies):
    for copy in copies:
        copy.wait_recv()


def step_kernel(
    blocks, slabs, source, level, quadrant, pops, cot, w_in_rows, w_mid, w_out_rows,
    final, grad_pops, grads,
    fa, fb, ca, cb, x1, x2, e, h0a, h1a, h0b, h1b, a1, a0,
    sheets0, sheets1, sheets2, sheets3, recv0, recv1, recv2, recv3, tmp, ghosts, shifted, picks, w_in, w_in_t, w_out, w_out_t, w_mid_t, tall, sems,
):
    g = Grid()
    cells = x1.shape[1]
    hid = w_mid.shape[0]
    chunks = cells // CHUNK
    for ref in (recv0, recv1, recv2, recv3):
        ref[:, SHEET:, :] = jnp.zeros((ref.shape[0], SHEET_ROWS - SHEET, LANES), F32)
    link = Exchange(blocks, slabs)
    link.greet()
    slots = [slot_of(source, blocks, face) for face in (0, 1)]
    for ref in (fa, fb, cb):
        ref[Q * PITCH :, :] = jnp.zeros((ROWS - Q * PITCH, LANES), F32)
    tmp[...] = jnp.zeros(tmp.shape, F32)

    from_cells(ca, cot)
    build_picks(level, quadrant, picks, True, (0, 1, 2))
    send_bars(g, ca, tmp, sheets0, picks)
    link.meet()
    bars2 = link.send(sheets0, recv0, sems.at[0])

    padded_rows(w_in_rows, tall, w_in_t, w_in)
    padded_rows(w_out_rows, tall, w_out, w_out_t)
    from_cells(fa, pops)

    def forward(f, x, h0, h1):
        @pl.loop(0, chunks)
        def _(i):
            at = span(i)
            state = get_lines(f, i)
            inputs = state.astype(BF16)
            x[:, at] = inputs
            first = jnp.tanh(mm(w_in[...], inputs)).astype(BF16)
            h0[:, at] = first
            second = jnp.tanh(mm(w_mid[...], first)).astype(BF16)
            h1[:, at] = second
            put_lines(f, i, state + mm(w_out[...], second))

    def backward(p, h0, h1):
        @pl.loop(0, chunks)
        def _(i):
            at = span(i)
            bar = get_lines(p, i)
            err = bar.astype(BF16)
            e[:, at] = err
            second = (mm(w_out_t[...], err) * slope(h1[:, at])).astype(BF16)
            a1[:, at] = second
            first = (mm(w_mid_t[...], second) * slope(h0[:, at])).astype(BF16)
            a0[:, at] = first
            put_lines(p, i, bar + mm(w_in_t[...], first))

    def weights(x, h0, h1, old):
        for at, left, right in (
            (0, a1.at[: hid // 2], h0),
            (hid // 2, a1.at[hid // 2 :], h0),
            (hid, x, a0),
            (hid + R, e, h1),
        ):
            value = outer(left[...], right[...])
            spot_rows = pl.ds(at, value.shape[0])
            grads[spot_rows] = grads[spot_rows] + value if old else value

    forward(fa, x1, h0a, h1a)
    gather_sheets(g, fa, sheets1)
    posts1 = link.send(sheets1, recv1, sems.at[1])
    w_mid_t[...] = w_mid[...].astype(F32).T.astype(BF16)
    build_picks(level, quadrant, picks, False, (1, 2))
    arrive(bars2)
    stream_back(g, ca, recv0, slots, functools.partial(save, cb))
    arrive(posts1)
    settle(recv1, slots, picks, fa, ghosts)
    stream(g, fa, ghosts, shifted, functools.partial(save, fb))

    forward(fb, x2, h0b, h1b)
    gather_sheets(g, fb, sheets2)
    posts2 = link.send(sheets2, recv2, sems.at[2])
    backward(cb, h0b, h1b)
    send_bars(g, cb, tmp, sheets3, picks)
    bars1 = link.send(sheets3, recv3, sems.at[3])
    grads[...] = jnp.zeros(grads.shape, F32)
    weights(x2, h0b, h1b, False)
    arrive(posts2)
    settle(recv2, slots, picks, fb, ghosts)
    stream(g, fb, ghosts, shifted, functools.partial(to_cells, final))
    arrive(bars1)
    stream_back(g, cb, recv3, slots, functools.partial(save, fa))
    backward(fa, h0a, h1a)
    weights(x1, h0a, h1a, True)
    for q in range(Q):
        for half in range(HALVES):
            to_cells(grad_pops, q, half, load(fa, q, half))
    for copies in (bars2, posts1, posts2, bars1):
        for copy in copies:
            copy.wait_send()


PIECES = 3


def sum_kernel(chips, slabs, grads, out, land_c, half, land_t, part, land_s, sems):
    me, level = lax.axis_index("blocks"), lax.axis_index("slab")
    core, chip = lax.rem(me, 2), me // 2
    rows, width = part.shape[1], land_s.shape[-1]
    peer_t = [lax.rem(chip + d, chips) for d in range(1, chips)]
    peer_s = [lax.rem(level + d, slabs) for d in range(1, slabs)]
    twin = {"blocks": me + 1 - 2 * core}
    sides = [{"blocks": 2 * t + core} for t in peer_t]
    stack = [{"slab": t} for t in peer_s]
    barrier = pltpu.get_barrier_semaphore()
    for device in [twin] + sides + stack:
        pl.semaphore_signal(barrier, inc=1, device_id=device, device_id_type=MESH)
    pl.semaphore_wait(barrier, 1 + len(sides) + len(stack))

    def send(src, dst, p, which, device):
        copy = pltpu.make_async_remote_copy(
            src_ref=src, dst_ref=dst, send_sem=sems.at[0, p, which], recv_sem=sems.at[1, p, which],
            device_id=device, device_id_type=MESH,
        )
        copy.start()
        return copy

    def half_of(p, c):
        return pl.ds(pl.multiple_of((2 * p + c) * chips * rows, 8), chips * rows)

    def row_of(p):
        return pl.ds(pl.multiple_of(((2 * p + core) * chips + chip) * rows, 8), rows)

    def lane_of(i):
        return pl.ds(pl.multiple_of(i * width, 128), width)

    first_t, first_s = 1, len(sides) + 1
    again = len(sides) + len(stack) + 1
    flying = [[] for _ in range(PIECES)]
    sent = []

    def stage(p, number):
        for copy in flying[p]:
            copy.wait_recv()
        sent.extend(flying[p])
        flying[p] = []
        if number == 0:
            flying[p] = [send(grads.at[half_of(p, 1 - core)], land_c.at[p], p, 0, twin)]
        if number == 1:
            half[p] = grads[half_of(p, core)] + land_c[p]
            flying[p] = [
                send(half.at[p, pl.ds(pl.multiple_of(t * rows, 8), rows)], land_t.at[p, i], p, first_t + i, device)
                for i, (t, device) in enumerate(zip(peer_t, sides))
            ]
        if number == 2:
            total = half[p, pl.ds(pl.multiple_of(chip * rows, 8), rows)]
            for i in range(len(sides)):
                total += land_t[p, i]
            part[p] = total
            flying[p] = [
                send(part.at[p, :, lane_of(t)], land_s.at[p, i], p, first_s + i, device)
                for i, (t, device) in enumerate(zip(peer_s, stack))
            ]
        if number == 3:
            mine = part[p, :, lane_of(level)]
            for i in range(len(stack)):
                mine += land_s[p, i]
            out[row_of(p), lane_of(level)] = mine
            spot = out.at[row_of(p), lane_of(level)]
            flying[p] = [send(spot, spot, p, again + first_s + i, device) for i, device in enumerate(stack)]
        if number == 4:
            spot = out.at[row_of(p)]
            flying[p] = [send(spot, spot, p, again + first_t + i, device) for i, device in enumerate(sides)]
        if number == 5:
            spot = out.at[half_of(p, core)]
            flying[p] = [send(spot, spot, p, again, twin)]

    for number in (0, 1):
        for p in range(PIECES):
            stage(p, number)
    for tick in range(2, 5 + PIECES + 2):
        for p in range(PIECES):
            number = tick - p
            if 2 <= number <= 6:
                stage(p, number)
    for copy in sent:
        copy.wait_send()


def vmem(count):
    return [pl.BlockSpec(memory_space=pltpu.VMEM)] * count


SMEM_SPEC = pl.BlockSpec(memory_space=pltpu.SMEM)
LIMIT = 60 * 1024 * 1024


def shape(dims, dtype=F32):
    return jax.ShapeDtypeStruct(dims, dtype)


def shards(blocks, slabs, populations, w_in, w_mid, w_out, cotangent, face_source, face_level, face_quadrant):
    cells = populations.shape[-1]
    hid = w_in.shape[0]
    pops, cot = (v.reshape(Q * cells // LANES, LANES) for v in (populations, cotangent))
    w_mid = w_mid[0]
    step = 8 * blocks * PIECES
    total_rows = -(-(hid + 2 * R) // step) * step
    volume = pltpu.VMEM((ROWS, LANES), F32)
    thin = pltpu.VMEM((R, cells), BF16)
    deep = pltpu.VMEM((hid, cells), BF16)
    slots = 2 * REACH + 3
    final, grad_pops, grads = pl.pallas_call(
        functools.partial(step_kernel, blocks, slabs),
        out_shape=(shape(pops.shape), shape(pops.shape), shape((total_rows, hid))),
        in_specs=[SMEM_SPEC] * 3 + vmem(5),
        out_specs=tuple(vmem(3)),
        scratch_shapes=[volume] * 4 + [thin] * 3 + [deep] * 6 + [
            *[pltpu.VMEM((3, SHEET_ROWS, LANES), F32)] * 4,
            *[pltpu.VMEM((slots, SHEET_ROWS, LANES), F32)] * 4,
            pltpu.VMEM((3, SHEET_ROWS, LANES), F32),
            pltpu.VMEM((4 * HALVES * 8, LANES), F32),
            pltpu.VMEM((16 * BLOCK, LANES), F32),
            pltpu.VMEM((10, A, A), BF16),
            pltpu.VMEM((hid, R), BF16),
            pltpu.VMEM((R, hid), BF16),
            pltpu.VMEM((R, hid), BF16),
            pltpu.VMEM((hid, R), BF16),
            pltpu.VMEM((hid, hid), BF16),
            pltpu.VMEM((R, hid), F32),
            pltpu.SemaphoreType.DMA((4, 2, slots)),
        ],
        compiler_params=pltpu.CompilerParams(vmem_limit_bytes=LIMIT, collective_id=0, has_side_effects=True),
        name="step",
    )(face_source.T, face_level, face_quadrant, pops, cot, w_in.T, w_mid, w_out)
    chips = blocks // 2
    rows, width = total_rows // (blocks * PIECES), hid // slabs
    total = pl.pallas_call(
        functools.partial(sum_kernel, chips, slabs),
        out_shape=shape((total_rows, hid)),
        in_specs=vmem(1),
        out_specs=vmem(1)[0],
        scratch_shapes=[
            pltpu.VMEM((PIECES, chips * rows, hid), F32),
            pltpu.VMEM((PIECES, chips * rows, hid), F32),
            pltpu.VMEM((PIECES, chips - 1, rows, hid), F32),
            pltpu.VMEM((PIECES, rows, hid), F32),
            pltpu.VMEM((PIECES, slabs - 1, rows, width), F32),
            pltpu.SemaphoreType.DMA((2, PIECES, 2 * (chips + slabs - 1))),
        ],
        compiler_params=pltpu.CompilerParams(collective_id=2, has_side_effects=True),
        name="sum_all",
    )(grads)
    total = total * float(blocks * slabs * cells) ** (-0.5)
    return (
        final.reshape(populations.shape),
        grad_pops.reshape(populations.shape),
        total[hid : hid + Q].T,
        total[:hid][None],
        total[hid + R : hid + R + Q],
    )


def solution(mesh):
    spread = P(None, "slab", "blocks", None)
    in_specs = (spread, P(), P(), P(), spread, P(), P("slab", "blocks", None), P("slab", "blocks", None))
    out_specs = (spread, spread, P(), P(), P())
    body = functools.partial(shards, mesh.shape["blocks"], mesh.shape["slab"])
    return jax.shard_map(body, mesh=mesh, in_specs=in_specs, out_specs=out_specs, check_vma=False)
```

```python
import functools

import jax
import jax.numpy as jnp
from jax import lax
from jax.experimental import pallas as pl
from jax.experimental.pallas import tpu as pltpu
from jax.sharding import PartitionSpec as P

REACH = 3
R = 24
S = 16
A = S * S
LANES = 128
HALVES = A // LANES
CHUNK = 1024
LINES = CHUNK // LANES
BLOCK = S + 2
PITCH = HALVES * BLOCK
ROWS = R * PITCH
MESH = pl.DeviceIdType.MESH
F32, BF16 = jnp.float32, jnp.bfloat16

VELOCITIES = [
    (0, 0, 0),
    (1, 0, 0),
    (-1, 0, 0),
    (0, 1, 0),
    (0, -1, 0),
    (0, 0, 1),
    (0, 0, -1),
    (1, 1, 0),
    (-1, -1, 0),
    (1, -1, 0),
    (-1, 1, 0),
    (1, 0, 1),
    (-1, 0, -1),
    (1, 0, -1),
    (-1, 0, 1),
    (0, 1, 1),
    (0, -1, -1),
    (0, 1, -1),
    (0, -1, 1),
]
Q = len(VELOCITIES)
OPPOSITE = [VELOCITIES.index((-a, -b, -c)) for a, b, c in VELOCITIES]
FACED = 5
SHEET = 2 * HALVES * FACED
SHEET_ROWS = 24


def members(axis, side):
    return [q for q, v in enumerate(VELOCITIES) if v[axis] == (1, -1)[side]]


def place(q, axis):
    side = 0 if VELOCITIES[q][axis] == 1 else 1
    return side, members(axis, side).index(q)


def base(q, half):
    return q * PITCH + half * BLOCK + 1


def load(ref, q, half, off=0):
    return ref[pl.ds(base(q, half) + off, S), :]


def save(ref, q, half, value):
    ref[pl.ds(base(q, half), S), :] = value


def get_lines(ref, i):
    first = i * (LINES // HALVES)
    return jnp.concatenate(
        [ref[pl.ds(j % HALVES * BLOCK + 1 + j // HALVES + first, R, stride=PITCH), :] for j in range(LINES)], axis=1
    )


def put_lines(ref, i, value):
    first = i * (LINES // HALVES)
    for j in range(LINES):
        at = pl.ds(j % HALVES * BLOCK + 1 + j // HALVES + first, R, stride=PITCH)
        ref[at, :] = value[:, j * LANES : (j + 1) * LANES]


def from_cells(dst, src):
    for q in range(Q):
        for half in range(HALVES):
            save(dst, q, half, src[pl.ds(q * S * HALVES + half, S, stride=HALVES), :])


def to_cells(dst, q, half, value):
    dst[pl.ds(q * S * HALVES + half, S, stride=HALVES), :] = value


class Grid:
    def __init__(self):
        self.x = lax.broadcasted_iota(jnp.int32, (S, LANES), 0)
        self.lane = lax.broadcasted_iota(jnp.int32, (S, LANES), 1)
        self.y = self.lane // S
        self.z = self.lane % S
        self.lane1 = lax.broadcasted_iota(jnp.int32, (1, LANES), 1)
        self.y1, self.z1 = self.lane1 // S, self.lane1 % S


def roll(x, shift):
    shift %= LANES
    return x if shift == 0 else pltpu.roll(x, shift, 1)


def fan(x, shift, stride):
    return pltpu.roll(x, shift % LANES, 1, stride=stride, stride_axis=0)


def carry(g, pair, step, lane):
    if step == 1:
        return [pair[0], jnp.where(lane < LANES - S, pair[1], pair[0])]
    if step == -1:
        return [jnp.where(lane >= S, pair[0], pair[1]), pair[1]]
    return pair


def wide(row):
    return jnp.broadcast_to(row, (8, LANES))


def spread_y(row_of, side):
    shift = 0 if side == 0 else -(LANES - S)
    return jnp.concatenate([fan(wide(row_of(half)), shift, S) for half in range(HALVES)], axis=0)


def spread_z(g, row_of, z, dy):
    pair = carry(g, [row_of(half) for half in range(HALVES)], dy, g.lane1)
    return [
        jnp.concatenate([fan(wide(row), z - (S - 1) + S * dy + 8 * part, 1) for part in range(2)], axis=0) for row in pair
    ]


def total_rows(x):
    return jnp.sum(x, axis=0, keepdims=True)


def sheet_row(side, half, r):
    return (side * HALVES + half) * FACED + r


def put_row(ref, side, half, r, value):
    at = sheet_row(side, half, r)
    ref[at : at + 1, :] = value


def fold_y(x, high):
    shift = S if high else 0
    return [total_rows(fan(x[8 * part : 8 * part + 8], shift, S)) for part in range(2)]


def fold_z(x, z):
    return total_rows(sum(fan(x[8 * part : 8 * part + 8], 8 * part - z, 1) for part in range(2)))


def gather_sheets(g, post, sheets):
    for q, v in enumerate(VELOCITIES):
        if v[0]:
            side, r = place(q, 0)
            for half in range(HALVES):
                at = base(q, half) + (S - 1 if v[0] == 1 else 0)
                put_row(sheets.at[0], side, half, r, post[at : at + 1, :])
        if v[1]:
            side, r = place(q, 1)
            high = v[1] == 1
            x = jnp.where(g.y == (7 if high else 0), load(post, q, 1 if high else 0), 0.0)
            for part, row in enumerate(fold_y(x, high)):
                put_row(sheets.at[1], side, part, r, row)
        if v[2]:
            side, r = place(q, 2)
            z = S - 1 if v[2] == 1 else 0
            for half in range(HALVES):
                row = fold_z(jnp.where(g.z == z, load(post, q, half), 0.0), z)
                put_row(sheets.at[2], side, half, r, row)


def inside_z(z, dz):
    return z != (0 if dz == 1 else S - 1)


def gather_bars(g, bar, tmp):
    last = LANES // S - 1
    for q, (dx, dy, dz) in enumerate(VELOCITIES):
        if dx:
            side, r = place(q, 0)
            rows = []
            for half in range(HALVES):
                at = base(q, half) + (0 if dx == 1 else S - 1)
                row = bar[at : at + 1, :]
                rows.append(jnp.where(inside_z(g.z1, dz), row, 0.0) if dz else row)
            rows = [roll(row, -S * dy - dz) for row in carry(g, rows, -dy, g.lane1)]
            if dy:
                half, y = (1, last) if dy == 1 else (0, 0)
                rows[half] = jnp.where(g.y1 == y, 0.0, rows[half])
            for half in range(HALVES):
                put_row(tmp.at[0], side, half, r, rows[half])
        if dy:
            side, r = place(q, 1)
            keep = g.y == (0 if dy == 1 else last)
            if dz:
                keep &= inside_z(g.z, dz)
            if dx:
                keep &= g.x != (S - 1 if dx == 1 else 0)
            x = jnp.where(keep, load(bar, q, 0 if dy == 1 else 1, dx), 0.0)
            for part, row in enumerate(fold_y(x, dy == -1)):
                put_row(tmp.at[1], side, part, r, roll(row, -dz))
        if dz:
            side, r = place(q, 2)
            z = 0 if dz == 1 else S - 1
            rows = []
            for half in range(HALVES):
                keep = g.z == z
                if dx:
                    keep &= g.x != (S - 1 if dx == 1 else 0)
                if dy and half == (0 if dy == 1 else 1):
                    keep &= g.y != (0 if dy == 1 else last)
                rows.append(fold_z(jnp.where(keep, load(bar, q, half, dx), 0.0), z))
            rows = [roll(row, -S * dy) for row in carry(g, rows, -dy, g.lane1)]
            if dy:
                half, y = (1, last) if dy == 1 else (0, 0)
                rows[half] = jnp.where(g.y1 == y, 0.0, rows[half])
            for half in range(HALVES):
                put_row(tmp.at[2], side, half, r, rows[half])


def refined(halves, pick, transposed):
    sheet = jnp.concatenate(halves, axis=1)
    hi = sheet.astype(BF16).astype(F32)
    rest = sheet - hi
    mid = rest.astype(BF16).astype(F32)
    parts = jnp.concatenate([hi, mid, rest - mid], axis=0).astype(BF16)
    dims = (((1,), (1 if transposed else 0,)), ((), ()))
    r = lax.dot_general(parts, pick, dims, preferred_element_type=F32)
    return r[:8] + r[8:16] + r[16:]


def sheet_halves(ref, side):
    return [ref[pl.ds(sheet_row(side, half, 0), 8), :] for half in range(HALVES)]


def send_bars(g, bar, tmp, sheets, picks):
    gather_bars(g, bar, tmp)
    for axis in range(3):
        for side in range(2):
            out = refined(sheet_halves(tmp.at[axis], side), picks[pick_at(axis, side, True)], True)
            for half in range(HALVES):
                sheets[axis, pl.ds(sheet_row(side, half, 0), FACED), :] = out[:FACED, half * LANES : (half + 1) * LANES]


def pick_at(axis, side, back):
    if axis == 0:
        return side
    return 2 + 8 // 2 * back + 2 * (axis - 1) + side


def build_picks(level, quadrant, picks, back, axes):
    lane = lax.broadcasted_iota(jnp.int32, (1, A), 1)
    source = lax.broadcasted_iota(jnp.int32, (A, A), 0)
    half = S // 2

    def turned(axis, i):
        if axis == 0:
            return i
        if axis == 1:
            return i // LANES * LANES + (7 - i // S % 8) * S + i % S
        return i // S * S + (S - 1 - i % S)

    for axis in axes:
        for side in range(2):
            face = 2 * axis + 1 - side
            quad = quadrant[0, 0, face]
            first, second = quad // 2, quad % 2
            if axis == 2:
                first, second = second, first

            def wanted(i):
                fine = (first * half + i // S // 2) * S + second * half + i % S // 2
                return jnp.where(level[0, 0, face] == 1, fine, i)

            want = turned(axis, wanted(lane)) if back else wanted(turned(axis, lane))
            picks[pick_at(axis, side, back)] = jnp.where(source == want, 1.0, 0.0).astype(BF16)


def slot_of(source, blocks, face):
    me = lax.axis_index("blocks")
    distance = lax.rem(source[face, me] - me + blocks, blocks)
    distance = jnp.where(distance > blocks // 2, distance - blocks, distance)
    slot = jnp.where(distance < 0, distance + REACH, distance + REACH - 1)
    return jnp.clip(slot, 0, 2 * REACH - 1)


def ghost_row(axis, side, half, r):
    return (((axis - 1) * 2 + side) * HALVES + half) * 8 + r


def settle(recv, slots, picks, post, ghosts):
    for side in range(2):
        slot = slots[1 - side]
        halves = [recv[slot, pl.ds(sheet_row(side, half, 0), 8), :] for half in range(HALVES)]
        out = refined(halves, picks[pick_at(0, side, False)], False)
        for r, q in enumerate(members(0, side)):
            for half in range(HALVES):
                at = base(q, half) + (-1 if side == 0 else S)
                post[at : at + 1, :] = out[r : r + 1, half * LANES : (half + 1) * LANES]
    for axis in (1, 2):
        for side in range(2):
            slot = 2 * REACH if axis == 1 else 2 * REACH + (2 if side == 0 else 1)
            out = refined(sheet_halves(recv.at[slot], side), picks[pick_at(axis, side, False)], False)
            for half in range(HALVES):
                at = ghost_row(axis, side, half, 0)
                ghosts[at : at + 8, :] = out[:, half * LANES : (half + 1) * LANES]


def stream(g, post, ghosts, shifted, store):
    last = LANES // S - 1
    used = [0]

    def moved(value, dx):
        if not dx:
            return value
        at = used[0] * BLOCK + 1
        used[0] += 1
        shifted[pl.ds(at, S), :] = value
        return shifted[pl.ds(at - dx, S), :]

    for q, (dx, dy, dz) in enumerate(VELOCITIES):
        t = [load(post, q, half, -dx) for half in range(HALVES)]
        if dy:
            side, r = place(q, 1)

            def row_y(half):
                at = ghost_row(1, side, half, r)
                return ghosts[at : at + 1, :]

            halo = moved(spread_y(row_y, side), dx)
            if dy == 1:
                inner = g.lane < LANES - S
                t = [jnp.where(inner, t[0], halo), jnp.where(inner, t[1], t[0])]
            else:
                inner = g.lane >= S
                t = [jnp.where(inner, t[0], t[1]), jnp.where(inner, t[1], halo)]
        t = [roll(x, S * dy + dz) for x in t]
        if dz:
            side, r = place(q, 2)
            z = 0 if dz == 1 else S - 1

            def row_z(half):
                at = ghost_row(2, side, half, r)
                return ghosts[at : at + 1, :]

            halo = [moved(x, dx) for x in spread_z(g, row_z, z, dy)]
            t = [jnp.where(g.z == z, halo[half], t[half]) for half in range(HALVES)]
        for half in range(HALVES):
            two = crossed(g, half, dx, dy, dz)
            if two is not None:
                t[half] = jnp.where(two, load(post, OPPOSITE[q], half), t[half])
            store(q, half, t[half])


def crossed(g, half, dx, dy, dz):
    if (dx != 0) + (dy != 0) + (dz != 0) < 2:
        return None
    if dy and half != (0 if dy == 1 else 1):
        return None
    on = None
    for d, c, top in ((dx, g.x, S - 1), (dy, g.y, LANES // S - 1), (dz, g.z, S - 1)):
        if d:
            hit = c == (0 if d == 1 else top)
            on = hit if on is None else on & hit
    return on


def stream_back(g, bar, recv, slots, store):
    last = LANES // S - 1
    for q, (dx, dy, dz) in enumerate(VELOCITIES):
        t = [load(bar, q, half, dx) for half in range(HALVES)]
        t = [roll(x, -S * dy - dz) for x in carry(g, t, -dy, g.lane)]
        faces = []
        if dx:
            side, r = place(q, 0)
            slot = slots[side]
            rows = [recv[slot, pl.ds(sheet_row(side, half, r), 1), :] for half in range(HALVES)]
            rows = [jnp.broadcast_to(row, (S, LANES)) for row in rows]
            faces.append((rows, [g.x == (S - 1 if dx == 1 else 0)] * 2))
        if dy:
            side, r = place(q, 1)
            full = spread_y(lambda half: recv[2 * REACH, pl.ds(sheet_row(side, half, r), 1), :], side)
            mask = g.y == (last if dy == 1 else 0)
            faces.append(([full, full], [mask if half == (1 if dy == 1 else 0) else None for half in range(HALVES)]))
        if dz:
            side, r = place(q, 2)
            slot = 2 * REACH + (1 if side == 0 else 2)
            z = S - 1 if dz == 1 else 0
            full = spread_z(g, lambda half: recv[slot, pl.ds(sheet_row(side, half, r), 1), :], z, 0)
            faces.append((full, [g.z == z] * 2))
        for half in range(HALVES):
            here = [(value[half], mask[half]) for value, mask in faces if mask[half] is not None]
            out = t[half]
            if len(here) == 1:
                out = jnp.where(here[0][1], here[0][0], out)
            if len(here) == 2:
                (va, ma), (vb, mb) = here
                both = va + vb + load(bar, OPPOSITE[q], half)
                out = jnp.where(mb, jnp.where(ma, both, vb), jnp.where(ma, va, out))
            store(q, half, out)


def mm(a, b):
    return jnp.dot(a, b, preferred_element_type=F32)


def outer(a, b):
    return lax.dot_general(a, b, (((1,), (1,)), ((), ())), preferred_element_type=F32)


def damp(u, h):
    wide_h = h.astype(F32)
    return (u * (1.0 - wide_h * wide_h)).astype(BF16)


def span(i):
    return pl.ds(pl.multiple_of(i * CHUNK, CHUNK), CHUNK)


def padded_rows(src, tall, flat, flipped):
    tall[...] = jnp.zeros(tall.shape, F32)
    tall[:Q] = src[...].astype(F32)
    flat[...] = tall[...].astype(BF16)
    flipped[...] = tall[...].T.astype(BF16)


BIG = 4
STAGES = 6


class Total:
    def __init__(self, blocks, slabs, hid, grads, out, land_c, half, land_a, tile, land_z, sems, scale):
        self.me, self.level = lax.axis_index("blocks"), lax.axis_index("slab")
        self.chips, self.pairs, self.scale = blocks // 2, slabs // 2, scale
        self.count = self.chips * 2
        self.core, self.chip = lax.rem(self.me, 2), self.me // 2
        self.low, self.high = lax.rem(self.level, 2), self.level // 2
        self.at = self.chip * 2 + self.low
        self.grads, self.out, self.land_c, self.half = grads, out, land_c, half
        self.land_a, self.tile, self.land_z, self.sems = land_a, tile, land_z, sems
        self.hid = hid
        self.rows = piece_rows(blocks, hid)
        self.first = [sum(2 * n for n in self.rows[:p]) for p in range(len(self.rows))]
        self.flying = [[] for _ in self.rows]
        self.done = []

    def go(self, p, src, dst, which, device):
        copy = pltpu.make_async_remote_copy(
            src_ref=src, dst_ref=dst, send_sem=self.sems.at[0, p, which], recv_sem=self.sems.at[1, p, which],
            device_id=device, device_id_type=MESH,
        )
        copy.start()
        self.flying[p].append(copy)
        self.done.append(copy)

    def settle(self, p):
        for copy in self.flying[p]:
            copy.wait_recv()
        self.flying[p] = []

    def rows_of(self, p, core):
        n = self.rows[p]
        return pl.ds(pl.multiple_of(self.first[p] + core * n, 8), n)

    def size(self, p):
        return part_size(self.rows[p], self.count, self.hid)

    def part(self, p, t, start):
        n, w = self.size(p)
        across = self.hid // w
        rows = pl.ds(pl.multiple_of(start + t // across * n, 8), n)
        return rows, pl.ds(pl.multiple_of(lax.rem(t, across) * w, 128), w)

    def twin(self):
        return {"blocks": self.me + 1 - 2 * self.core}

    def near(self):
        for d in range(1, self.count):
            t = lax.rem(self.at + d, self.count)
            yield d - 1, t, {"blocks": t // 2 * 2 + self.core, "slab": self.high * 2 + lax.rem(t, 2)}

    def far(self):
        for d in range(1, self.pairs):
            yield d - 1, {"slab": lax.rem(self.high + d, self.pairs) * 2 + self.low}

    def friends(self):
        return [device for _, _, device in self.near()] + [device for _, device in self.far()]

    def stage(self, p, number):
        n, w = self.size(p)
        whole, small = pl.ds(0, self.rows[p]), (pl.ds(0, n), pl.ds(0, w))
        tile = self.tile.at[p, *small]
        again = self.count + self.pairs
        start = self.first[p] + self.core * self.rows[p]
        self.settle(p)
        if number == 0:
            self.go(p, self.grads.at[self.rows_of(p, 1 - self.core)], self.land_c.at[p, whole], 0, self.twin())
        elif number == 1:
            self.half[p, whole] = self.grads[self.rows_of(p, self.core)] + self.land_c[p, whole]
            for i, t, device in self.near():
                self.go(p, self.half.at[p, *self.part(p, t, 0)], self.land_a.at[p, i, *small], 1 + i, device)
        elif number == 2:
            total = self.half[p, *self.part(p, self.at, 0)]
            for i in range(self.count - 1):
                total += self.land_a[p, i, *small]
            tile[...] = total
            for i, device in self.far():
                self.go(p, tile, self.land_z.at[p, i, *small], self.count + i, device)
        elif number == 3:
            total = tile[...]
            for i in range(self.pairs - 1):
                total += self.land_z[p, i, *small]
            spot = self.out.at[*self.part(p, self.at, start)]
            spot[...] = total * self.scale
            for i, t, device in self.near():
                self.go(p, spot, spot, again + i, device)
        elif number == 4:
            rows = self.out.at[self.rows_of(p, self.core)]
            self.go(p, rows, rows, again + self.count, self.twin())

    def close(self):
        for copy in self.done:
            copy.wait_send()


def piece_rows(blocks, hid):
    return [hid // BIG // 2] * BIG + [max(R + 8, blocks * 8 * LANES // hid)]


def part_size(rows, count, hid):
    n = max(rows // count, 8)
    return n, rows // n * hid // count


OFFSETS = [d for d in range(-REACH, REACH + 1) if d != 0]


class Exchange:
    def __init__(self, blocks, slabs):
        me, level = lax.axis_index("blocks"), lax.axis_index("slab")
        self.side = [lax.rem(me - d + blocks, blocks) for d in OFFSETS]
        self.other = me + 1 - 2 * lax.rem(me, 2)
        self.above, self.below = lax.rem(level + 1, slabs), lax.rem(level + slabs - 1, slabs)
        self.friends = []

    def greet(self):
        barrier = pltpu.get_barrier_semaphore()
        for target in self.side:
            pl.semaphore_signal(barrier, inc=1, device_id={"blocks": target}, device_id_type=MESH)
        for target in (self.above, self.below):
            pl.semaphore_signal(barrier, inc=1, device_id={"slab": target}, device_id_type=MESH)
        for device in self.friends:
            pl.semaphore_signal(barrier, inc=1, device_id=device, device_id_type=MESH)

    def meet(self):
        pl.semaphore_wait(pltpu.get_barrier_semaphore(), len(self.side) + 2 + len(self.friends))

    def send(self, sheets, recv, sems):
        plan = [(0, i, {"blocks": target}) for i, target in enumerate(self.side)]
        plan.append((1, 2 * REACH, {"blocks": self.other}))
        plan.append((2, 2 * REACH + 1, {"slab": self.below}))
        plan.append((2, 2 * REACH + 2, {"slab": self.above}))
        copies = []
        for which, slot, device in sorted(plan, key=lambda row: -row[0]):
            copy = pltpu.make_async_remote_copy(
                src_ref=sheets.at[which, pl.ds(0, SHEET)], dst_ref=recv.at[slot, pl.ds(0, SHEET)],
                send_sem=sems.at[0, slot], recv_sem=sems.at[1, slot],
                device_id=device, device_id_type=MESH,
            )
            copy.start()
            copies.append(copy)
        return copies


def arrive(copies):
    for copy in copies:
        copy.wait_recv()


def step_kernel(
    blocks, slabs, source, level, quadrant, pops_hbm, cot_hbm, w_in_hbm, w_mid_hbm, w_out_hbm,
    final, grad_pops, out,
    grads, land_c, half_c, land_a, tile, land_z, total_sems, fa, fb, ca, cb, x1, x2, e, h0a, h1a, h0b, h1b, a1, a0, u,
    sheets0, sheets1, sheets2, sheets3, recv0, recv1, recv2, recv3, tmp, ghosts, shifted, picks, w_in, w_in_t, w_out, w_out_t, w_mid_t, tall,
    pops, cot, w_in_rows, w_mid, w_out_rows, load_sems, sems,
):
    loads = [
        pltpu.make_async_copy(src, dst, load_sems.at[i])
        for i, (src, dst) in enumerate(
            ((cot_hbm, cot), (pops_hbm, pops), (w_in_hbm, w_in_rows), (w_out_hbm, w_out_rows), (w_mid_hbm, w_mid))
        )
    ]
    for copy in loads:
        copy.start()
    g = Grid()
    cells = x1.shape[1]
    hid = w_mid.shape[0]
    chunks = cells // CHUNK
    for ref in (recv0, recv1, recv2, recv3):
        ref[:, SHEET:, :] = jnp.zeros((ref.shape[0], SHEET_ROWS - SHEET, LANES), F32)
    link = Exchange(blocks, slabs)
    total = Total(
        blocks, slabs, hid, grads, out, land_c, half_c, land_a, tile, land_z, total_sems,
        float(blocks * slabs * cells) ** (-0.5),
    )
    link.friends = total.friends()
    second = hid + total.rows[BIG]
    link.greet()
    slots = [slot_of(source, blocks, face) for face in (0, 1)]
    for ref in (fa, fb, cb):
        ref[Q * PITCH :, :] = jnp.zeros((ROWS - Q * PITCH, LANES), F32)
    tmp[...] = jnp.zeros(tmp.shape, F32)

    build_picks(level, quadrant, picks, True, (0, 1, 2))
    loads[0].wait()
    from_cells(ca, cot)
    send_bars(g, ca, tmp, sheets0, picks)
    link.meet()
    bars2 = link.send(sheets0, recv0, sems.at[0])

    for copy in loads[1:]:
        copy.wait()
    padded_rows(w_in_rows, tall, w_in_t, w_in)
    padded_rows(w_out_rows, tall, w_out, w_out_t)
    from_cells(fa, pops)

    def forward(f, x, h0, h1):
        @pl.loop(0, chunks)
        def _(i):
            at = span(i)
            state = get_lines(f, i)
            inputs = state.astype(BF16)
            x[:, at] = inputs
            first = jnp.tanh(mm(w_in[...], inputs)).astype(BF16)
            h0[:, at] = first
            second = jnp.tanh(mm(w_mid[...], first)).astype(BF16)
            h1[:, at] = second
            put_lines(f, i, state + mm(w_out[...], second))

    def backward(p, h0, h1):
        @pl.loop(0, chunks)
        def _(i):
            at = span(i)
            bar = get_lines(p, i)
            second = damp(u[:, at], h1[:, at])
            a1[:, at] = second
            first = damp(mm(w_mid_t[...], second), h0[:, at])
            a0[:, at] = first
            put_lines(p, i, bar + mm(w_in_t[...], first))

    def lift(p):
        @pl.loop(0, chunks)
        def _(i):
            at = span(i)
            err = get_lines(p, i).astype(BF16)
            e[:, at] = err
            u[:, at] = mm(w_out_t[...], err)

    def top_down(h1, first, count):
        rows = pl.ds(first, count)

        @pl.loop(0, chunks)
        def _(i):
            at = span(i)
            a1[rows, at] = damp(mm(w_out_t[rows], e[:, at]), h1[rows, at])

    def bottom(p, h0, i):
        at = pl.ds(i * CHUNK, CHUNK)
        first = damp(mm(w_mid_t[...], a1[:, at]), h0[:, at])
        a0[:, at] = first
        put_lines(p, i, get_lines(p, i) + mm(w_in_t[...], first))

    def weigh(first, left, right, old, columns=None):
        value = outer(left[...], right[...])
        spot_rows = pl.ds(first, value.shape[0])
        at = (spot_rows, columns or slice(None))
        grads[at] = grads[at] + value if old else value

    forward(fa, x1, h0a, h1a)
    gather_sheets(g, fa, sheets1)
    posts1 = link.send(sheets1, recv1, sems.at[1])
    w_mid_t[...] = w_mid[...].astype(F32).T.astype(BF16)
    build_picks(level, quadrant, picks, False, (1, 2))
    arrive(bars2)
    stream_back(g, ca, recv0, slots, functools.partial(save, cb))
    lift(cb)
    arrive(posts1)
    settle(recv1, slots, picks, fa, ghosts)
    stream(g, fa, ghosts, shifted, functools.partial(save, fb))

    forward(fb, x2, h0b, h1b)
    gather_sheets(g, fb, sheets2)
    posts2 = link.send(sheets2, recv2, sems.at[2])
    backward(cb, h0b, h1b)
    send_bars(g, cb, tmp, sheets3, picks)
    bars1 = link.send(sheets3, recv3, sems.at[3])
    mid = hid // 2
    grads[hid:] = jnp.zeros((grads.shape[0] - hid, hid), F32)
    weigh(0, a1.at[:mid], h0b, False)
    weigh(mid, a1.at[mid:], h0b, False)
    weigh(hid, x2, a0, False)
    weigh(second, e, h1b, False)
    arrive(posts2)
    settle(recv2, slots, picks, fb, ghosts)
    stream(g, fb, ghosts, shifted, functools.partial(to_cells, final))
    arrive(bars1)
    stream_back(g, cb, recv3, slots, functools.partial(save, fa))
    for i in range(chunks):
        e[:, i * CHUNK : (i + 1) * CHUNK] = get_lines(fa, i).astype(BF16)

    def turns(*pairs):
        pairs = pairs if isinstance(pairs[0], tuple) else (pairs,)
        for p, number in pairs:
            total.stage(p, number)

    top_down(h1a, 0, mid)
    weigh(0, a1.at[:mid], h0a, True)
    turns((0, 0), (1, 0))
    top_down(h1a, mid, mid)
    weigh(mid, a1.at[mid:], h0a.at[:mid], True, slice(0, mid))
    turns((0, 1), (1, 1))
    weigh(mid, a1.at[mid:], h0a.at[mid:], True, slice(mid, hid))
    turns((2, 0), (3, 0))
    weigh(second, e, h1a, True)
    turns((2, 1), (3, 1))
    for i in range(chunks):
        bottom(fa, h0a, i)
    weigh(hid, x1, a0, True)
    turns((BIG, 0))
    for q in range(Q):
        for half in range(HALVES):
            to_cells(grad_pops, q, half, load(fa, q, half))
    turns((0, 2), (1, 2), (BIG, 1), (2, 2), (3, 2))
    for number in range(3, STAGES):
        turns((0, number), (1, number), (2, number), (3, number), (BIG, number - 1))
    turns((BIG, STAGES - 1))
    total.close()
    for copies in (bars2, posts1, posts2, bars1):
        for copy in copies:
            copy.wait_send()


def leave_kernel(final, grad_pops, total, final_out, pops_out, mid_out, in_out, out_out, first_small, second_small, sems):
    hid = mid_out.shape[0]
    second = total.shape[0] - (total.shape[0] - hid) // 2
    first_small[...] = total[hid : hid + Q, :]
    second_small[...] = total[second : second + Q, :]
    plan = [
        (total.at[pl.ds(0, hid)], mid_out),
        (final, final_out),
        (grad_pops, pops_out),
        (first_small, in_out),
        (second_small, out_out),
    ]
    copies = [pltpu.make_async_copy(src, dst, sems.at[i]) for i, (src, dst) in enumerate(plan)]
    for copy in copies:
        copy.start()
    for copy in copies:
        copy.wait()


def vmem(count):
    return [pl.BlockSpec(memory_space=pltpu.VMEM)] * count


SMEM_SPEC = pl.BlockSpec(memory_space=pltpu.SMEM)
LIMIT = 50 * 1024 * 1024


def shape(dims, dtype=F32):
    return jax.ShapeDtypeStruct(dims, dtype)


def shards(blocks, slabs, populations, w_in, w_mid, w_out, cotangent, face_source, face_level, face_quadrant):
    cells = populations.shape[-1]
    hid = w_in.shape[0]
    pops, cot = (v.reshape(Q * cells // LANES, LANES) for v in (populations, cotangent))
    w_mid = w_mid[0]
    pieces = piece_rows(blocks, hid)
    rows, most = 2 * sum(pieces), max(pieces)
    sizes = [part_size(n, blocks, hid) for n in pieces]
    small = tuple(max(size[axis] for size in sizes) for axis in range(2))
    pieces = len(pieces)
    volume = pltpu.VMEM((ROWS, LANES), F32)
    thin = pltpu.VMEM((R, cells), BF16)
    deep = pltpu.VMEM((hid, cells), BF16)
    slots = 2 * REACH + 3
    final, grad_pops, total = pl.pallas_call(
        functools.partial(step_kernel, blocks, slabs),
        out_shape=(shape(pops.shape), shape(pops.shape), shape((rows, hid))),
        in_specs=[SMEM_SPEC] * 3 + [pl.BlockSpec(memory_space=pltpu.HBM)] * 5,
        out_specs=tuple(vmem(3)),
        scratch_shapes=[
            pltpu.VMEM((rows, hid), F32),
            pltpu.VMEM((pieces, most, hid), F32),
            pltpu.VMEM((pieces, most, hid), F32),
            pltpu.VMEM((pieces, blocks - 1, *small), F32),
            pltpu.VMEM((pieces, *small), F32),
            pltpu.VMEM((pieces, max(slabs // 2 - 1, 1), *small), F32),
            pltpu.SemaphoreType.DMA((2, pieces, 2 * blocks + slabs // 2 + 1)),
        ] + [volume] * 4 + [thin] * 3 + [deep] * 6 + [pltpu.VMEM((hid, cells), F32)] + [
            *[pltpu.VMEM((3, SHEET_ROWS, LANES), F32)] * 4,
            *[pltpu.VMEM((slots, SHEET_ROWS, LANES), F32)] * 4,
            pltpu.VMEM((3, SHEET_ROWS, LANES), F32),
            pltpu.VMEM((4 * HALVES * 8, LANES), F32),
            pltpu.VMEM((16 * BLOCK, LANES), F32),
            pltpu.VMEM((10, A, A), BF16),
            pltpu.VMEM((hid, R), BF16),
            pltpu.VMEM((R, hid), BF16),
            pltpu.VMEM((R, hid), BF16),
            pltpu.VMEM((hid, R), BF16),
            pltpu.VMEM((hid, hid), BF16),
            pltpu.VMEM((R, hid), F32),
            pltpu.VMEM(pops.shape, F32),
            pltpu.VMEM(cot.shape, F32),
            pltpu.VMEM((Q, hid), BF16),
            pltpu.VMEM((hid, hid), BF16),
            pltpu.VMEM((Q, hid), BF16),
            pltpu.SemaphoreType.DMA((5,)),
            pltpu.SemaphoreType.DMA((4, 2, slots)),
        ],
        compiler_params=pltpu.CompilerParams(vmem_limit_bytes=LIMIT, collective_id=0, has_side_effects=True),
        name="step",
    )(*[
        pltpu.with_memory_space_constraint(v, pltpu.HBM)
        for v in (face_source.T, face_level, face_quadrant, pops, cot, w_in.T, w_mid, w_out)
    ])
    final, grad_pops, grad_mid, grad_in, grad_out = pl.pallas_call(
        leave_kernel,
        out_shape=(
            shape(pops.shape), shape(pops.shape), shape((hid, hid)), shape((Q, hid)), shape((Q, hid)),
        ),
        in_specs=vmem(3),
        out_specs=tuple([pl.BlockSpec(memory_space=pl.ANY)] * 5),
        scratch_shapes=[pltpu.VMEM((Q, hid), F32), pltpu.VMEM((Q, hid), F32), pltpu.SemaphoreType.DMA((5,))],
        compiler_params=pltpu.CompilerParams(vmem_limit_bytes=4 * 1024 * 1024),
        name="leave",
    )(final, grad_pops, total)
    return (
        final.reshape(populations.shape),
        grad_pops.reshape(populations.shape),
        grad_in.T,
        grad_mid[None],
        grad_out,
    )


def solution(mesh):
    spread = P(None, "slab", "blocks", None)
    in_specs = (spread, P(), P(), P(), spread, P(), P("slab", "blocks", None), P("slab", "blocks", None))
    out_specs = (spread, spread, P(), P(), P())
    body = functools.partial(shards, mesh.shape["blocks"], mesh.shape["slab"])
    return jax.shard_map(body, mesh=mesh, in_specs=in_specs, out_specs=out_specs, check_vma=False)
```

```python
import functools

import jax
import jax.numpy as jnp
from jax import lax
from jax.experimental import pallas as pl
from jax.experimental.pallas import tpu as pltpu
from jax.sharding import PartitionSpec as P

REACH = 3
R = 24
S = 16
A = S * S
LANES = 128
HALVES = A // LANES
CHUNK = 1024
LINES = CHUNK // LANES
BLOCK = S + 2
PITCH = HALVES * BLOCK
ROWS = R * PITCH
MESH = pl.DeviceIdType.MESH
F32, BF16 = jnp.float32, jnp.bfloat16

VELOCITIES = [
    (0, 0, 0),
    (1, 0, 0),
    (-1, 0, 0),
    (0, 1, 0),
    (0, -1, 0),
    (0, 0, 1),
    (0, 0, -1),
    (1, 1, 0),
    (-1, -1, 0),
    (1, -1, 0),
    (-1, 1, 0),
    (1, 0, 1),
    (-1, 0, -1),
    (1, 0, -1),
    (-1, 0, 1),
    (0, 1, 1),
    (0, -1, -1),
    (0, 1, -1),
    (0, -1, 1),
]
Q = len(VELOCITIES)
OPPOSITE = [VELOCITIES.index((-a, -b, -c)) for a, b, c in VELOCITIES]
FACED = 5
SHEET = 2 * HALVES * FACED
SHEET_ROWS = 24


def members(axis, side):
    return [q for q, v in enumerate(VELOCITIES) if v[axis] == (1, -1)[side]]


def place(q, axis):
    side = 0 if VELOCITIES[q][axis] == 1 else 1
    return side, members(axis, side).index(q)


def base(q, half):
    return q * PITCH + half * BLOCK + 1


def load(ref, q, half, off=0):
    return ref[pl.ds(base(q, half) + off, S), :]


def save(ref, q, half, value):
    ref[pl.ds(base(q, half), S), :] = value


def get_lines(ref, i):
    first = i * (LINES // HALVES)
    return jnp.concatenate(
        [ref[pl.ds(j % HALVES * BLOCK + 1 + j // HALVES + first, R, stride=PITCH), :] for j in range(LINES)], axis=1
    )


def put_lines(ref, i, value):
    first = i * (LINES // HALVES)
    for j in range(LINES):
        at = pl.ds(j % HALVES * BLOCK + 1 + j // HALVES + first, R, stride=PITCH)
        ref[at, :] = value[:, j * LANES : (j + 1) * LANES]


def from_cells(dst, src):
    for q in range(Q):
        for half in range(HALVES):
            save(dst, q, half, src[pl.ds(q * S * HALVES + half, S, stride=HALVES), :])


def to_cells(dst, q, half, value):
    dst[pl.ds(q * S * HALVES + half, S, stride=HALVES), :] = value


class Grid:
    def __init__(self):
        self.x = lax.broadcasted_iota(jnp.int32, (S, LANES), 0)
        self.lane = lax.broadcasted_iota(jnp.int32, (S, LANES), 1)
        self.y = self.lane // S
        self.z = self.lane % S
        self.lane1 = lax.broadcasted_iota(jnp.int32, (1, LANES), 1)
        self.y1, self.z1 = self.lane1 // S, self.lane1 % S


def roll(x, shift):
    shift %= LANES
    return x if shift == 0 else pltpu.roll(x, shift, 1)


def fan(x, shift, stride):
    return pltpu.roll(x, shift % LANES, 1, stride=stride, stride_axis=0)


def carry(g, pair, step, lane):
    if step == 1:
        return [pair[0], jnp.where(lane < LANES - S, pair[1], pair[0])]
    if step == -1:
        return [jnp.where(lane >= S, pair[0], pair[1]), pair[1]]
    return pair


def wide(row):
    return jnp.broadcast_to(row, (8, LANES))


def spread_y(row_of, side):
    shift = 0 if side == 0 else -(LANES - S)
    return jnp.concatenate([fan(wide(row_of(half)), shift, S) for half in range(HALVES)], axis=0)


def spread_z(g, row_of, z, dy):
    pair = carry(g, [row_of(half) for half in range(HALVES)], dy, g.lane1)
    return [
        jnp.concatenate([fan(wide(row), z - (S - 1) + S * dy + 8 * part, 1) for part in range(2)], axis=0) for row in pair
    ]


def total_rows(x):
    return jnp.sum(x, axis=0, keepdims=True)


def sheet_row(side, half, r):
    return (side * HALVES + half) * FACED + r


def put_row(ref, side, half, r, value):
    at = sheet_row(side, half, r)
    ref[at : at + 1, :] = value


def fold_y(x, high):
    shift = S if high else 0
    return [total_rows(fan(x[8 * part : 8 * part + 8], shift, S)) for part in range(2)]


def fold_z(x, z):
    return total_rows(sum(fan(x[8 * part : 8 * part + 8], 8 * part - z, 1) for part in range(2)))


def gather_sheets(g, post, sheets):
    for q, v in enumerate(VELOCITIES):
        if v[0]:
            side, r = place(q, 0)
            for half in range(HALVES):
                at = base(q, half) + (S - 1 if v[0] == 1 else 0)
                put_row(sheets.at[0], side, half, r, post[at : at + 1, :])
        if v[1]:
            side, r = place(q, 1)
            high = v[1] == 1
            x = jnp.where(g.y == (7 if high else 0), load(post, q, 1 if high else 0), 0.0)
            for part, row in enumerate(fold_y(x, high)):
                put_row(sheets.at[1], side, part, r, row)
        if v[2]:
            side, r = place(q, 2)
            z = S - 1 if v[2] == 1 else 0
            for half in range(HALVES):
                row = fold_z(jnp.where(g.z == z, load(post, q, half), 0.0), z)
                put_row(sheets.at[2], side, half, r, row)


def inside_z(z, dz):
    return z != (0 if dz == 1 else S - 1)


def gather_bars(g, bar, tmp):
    last = LANES // S - 1
    for q, (dx, dy, dz) in enumerate(VELOCITIES):
        if dx:
            side, r = place(q, 0)
            rows = []
            for half in range(HALVES):
                at = base(q, half) + (0 if dx == 1 else S - 1)
                row = bar[at : at + 1, :]
                rows.append(jnp.where(inside_z(g.z1, dz), row, 0.0) if dz else row)
            rows = [roll(row, -S * dy - dz) for row in carry(g, rows, -dy, g.lane1)]
            if dy:
                half, y = (1, last) if dy == 1 else (0, 0)
                rows[half] = jnp.where(g.y1 == y, 0.0, rows[half])
            for half in range(HALVES):
                put_row(tmp.at[0], side, half, r, rows[half])
        if dy:
            side, r = place(q, 1)
            keep = g.y == (0 if dy == 1 else last)
            if dz:
                keep &= inside_z(g.z, dz)
            if dx:
                keep &= g.x != (S - 1 if dx == 1 else 0)
            x = jnp.where(keep, load(bar, q, 0 if dy == 1 else 1, dx), 0.0)
            for part, row in enumerate(fold_y(x, dy == -1)):
                put_row(tmp.at[1], side, part, r, roll(row, -dz))
        if dz:
            side, r = place(q, 2)
            z = 0 if dz == 1 else S - 1
            rows = []
            for half in range(HALVES):
                keep = g.z == z
                if dx:
                    keep &= g.x != (S - 1 if dx == 1 else 0)
                if dy and half == (0 if dy == 1 else 1):
                    keep &= g.y != (0 if dy == 1 else last)
                rows.append(fold_z(jnp.where(keep, load(bar, q, half, dx), 0.0), z))
            rows = [roll(row, -S * dy) for row in carry(g, rows, -dy, g.lane1)]
            if dy:
                half, y = (1, last) if dy == 1 else (0, 0)
                rows[half] = jnp.where(g.y1 == y, 0.0, rows[half])
            for half in range(HALVES):
                put_row(tmp.at[2], side, half, r, rows[half])


def refined(halves, pick, transposed):
    sheet = jnp.concatenate(halves, axis=1)
    hi = sheet.astype(BF16).astype(F32)
    rest = sheet - hi
    mid = rest.astype(BF16).astype(F32)
    parts = jnp.concatenate([hi, mid, rest - mid], axis=0).astype(BF16)
    dims = (((1,), (1 if transposed else 0,)), ((), ()))
    r = lax.dot_general(parts, pick, dims, preferred_element_type=F32)
    return r[:8] + r[8:16] + r[16:]


def sheet_halves(ref, side):
    return [ref[pl.ds(sheet_row(side, half, 0), 8), :] for half in range(HALVES)]


def send_bars(g, bar, tmp, sheets, picks):
    gather_bars(g, bar, tmp)
    for axis in range(3):
        for side in range(2):
            out = refined(sheet_halves(tmp.at[axis], side), picks[pick_at(axis, side, True)], True)
            for half in range(HALVES):
                sheets[axis, pl.ds(sheet_row(side, half, 0), FACED), :] = out[:FACED, half * LANES : (half + 1) * LANES]


def pick_at(axis, side, back):
    if axis == 0:
        return side
    return 2 + 8 // 2 * back + 2 * (axis - 1) + side


def build_picks(level, quadrant, picks, back, axes):
    lane = lax.broadcasted_iota(jnp.int32, (1, A), 1)
    source = lax.broadcasted_iota(jnp.int32, (A, A), 0)
    half = S // 2

    def turned(axis, i):
        if axis == 0:
            return i
        if axis == 1:
            return i // LANES * LANES + (7 - i // S % 8) * S + i % S
        return i // S * S + (S - 1 - i % S)

    for axis in axes:
        for side in range(2):
            face = 2 * axis + 1 - side
            quad = quadrant[0, 0, face]
            first, second = quad // 2, quad % 2
            if axis == 2:
                first, second = second, first

            def wanted(i):
                fine = (first * half + i // S // 2) * S + second * half + i % S // 2
                return jnp.where(level[0, 0, face] == 1, fine, i)

            want = turned(axis, wanted(lane)) if back else wanted(turned(axis, lane))
            picks[pick_at(axis, side, back)] = jnp.where(source == want, 1.0, 0.0).astype(BF16)


def slot_of(source, blocks, face):
    me = lax.axis_index("blocks")
    distance = lax.rem(source[face, me] - me + blocks, blocks)
    distance = jnp.where(distance > blocks // 2, distance - blocks, distance)
    slot = jnp.where(distance < 0, distance + REACH, distance + REACH - 1)
    return jnp.clip(slot, 0, 2 * REACH - 1)


def ghost_row(axis, side, half, r):
    return (((axis - 1) * 2 + side) * HALVES + half) * 8 + r


def settle(recv, slots, picks, post, ghosts):
    for side in range(2):
        slot = slots[1 - side]
        halves = [recv[slot, pl.ds(sheet_row(side, half, 0), 8), :] for half in range(HALVES)]
        out = refined(halves, picks[pick_at(0, side, False)], False)
        for r, q in enumerate(members(0, side)):
            for half in range(HALVES):
                at = base(q, half) + (-1 if side == 0 else S)
                post[at : at + 1, :] = out[r : r + 1, half * LANES : (half + 1) * LANES]
    for axis in (1, 2):
        for side in range(2):
            slot = 2 * REACH if axis == 1 else 2 * REACH + (2 if side == 0 else 1)
            out = refined(sheet_halves(recv.at[slot], side), picks[pick_at(axis, side, False)], False)
            for half in range(HALVES):
                at = ghost_row(axis, side, half, 0)
                ghosts[at : at + 8, :] = out[:, half * LANES : (half + 1) * LANES]


def stream(g, post, ghosts, shifted, store):
    last = LANES // S - 1
    used = [0]

    def moved(value, dx):
        if not dx:
            return value
        at = used[0] * BLOCK + 1
        used[0] += 1
        shifted[pl.ds(at, S), :] = value
        return shifted[pl.ds(at - dx, S), :]

    for q, (dx, dy, dz) in enumerate(VELOCITIES):
        t = [load(post, q, half, -dx) for half in range(HALVES)]
        if dy:
            side, r = place(q, 1)

            def row_y(half):
                at = ghost_row(1, side, half, r)
                return ghosts[at : at + 1, :]

            halo = moved(spread_y(row_y, side), dx)
            if dy == 1:
                inner = g.lane < LANES - S
                t = [jnp.where(inner, t[0], halo), jnp.where(inner, t[1], t[0])]
            else:
                inner = g.lane >= S
                t = [jnp.where(inner, t[0], t[1]), jnp.where(inner, t[1], halo)]
        t = [roll(x, S * dy + dz) for x in t]
        if dz:
            side, r = place(q, 2)
            z = 0 if dz == 1 else S - 1

            def row_z(half):
                at = ghost_row(2, side, half, r)
                return ghosts[at : at + 1, :]

            halo = [moved(x, dx) for x in spread_z(g, row_z, z, dy)]
            t = [jnp.where(g.z == z, halo[half], t[half]) for half in range(HALVES)]
        for half in range(HALVES):
            two = crossed(g, half, dx, dy, dz)
            if two is not None:
                t[half] = jnp.where(two, load(post, OPPOSITE[q], half), t[half])
            store(q, half, t[half])


def crossed(g, half, dx, dy, dz):
    if (dx != 0) + (dy != 0) + (dz != 0) < 2:
        return None
    if dy and half != (0 if dy == 1 else 1):
        return None
    on = None
    for d, c, top in ((dx, g.x, S - 1), (dy, g.y, LANES // S - 1), (dz, g.z, S - 1)):
        if d:
            hit = c == (0 if d == 1 else top)
            on = hit if on is None else on & hit
    return on


def stream_back(g, bar, recv, slots, store):
    last = LANES // S - 1
    for q, (dx, dy, dz) in enumerate(VELOCITIES):
        t = [load(bar, q, half, dx) for half in range(HALVES)]
        t = [roll(x, -S * dy - dz) for x in carry(g, t, -dy, g.lane)]
        faces = []
        if dx:
            side, r = place(q, 0)
            slot = slots[side]
            rows = [recv[slot, pl.ds(sheet_row(side, half, r), 1), :] for half in range(HALVES)]
            rows = [jnp.broadcast_to(row, (S, LANES)) for row in rows]
            faces.append((rows, [g.x == (S - 1 if dx == 1 else 0)] * 2))
        if dy:
            side, r = place(q, 1)
            full = spread_y(lambda half: recv[2 * REACH, pl.ds(sheet_row(side, half, r), 1), :], side)
            mask = g.y == (last if dy == 1 else 0)
            faces.append(([full, full], [mask if half == (1 if dy == 1 else 0) else None for half in range(HALVES)]))
        if dz:
            side, r = place(q, 2)
            slot = 2 * REACH + (1 if side == 0 else 2)
            z = S - 1 if dz == 1 else 0
            full = spread_z(g, lambda half: recv[slot, pl.ds(sheet_row(side, half, r), 1), :], z, 0)
            faces.append((full, [g.z == z] * 2))
        for half in range(HALVES):
            here = [(value[half], mask[half]) for value, mask in faces if mask[half] is not None]
            out = t[half]
            if len(here) == 1:
                out = jnp.where(here[0][1], here[0][0], out)
            if len(here) == 2:
                (va, ma), (vb, mb) = here
                both = va + vb + load(bar, OPPOSITE[q], half)
                out = jnp.where(mb, jnp.where(ma, both, vb), jnp.where(ma, va, out))
            store(q, half, out)


def mm(a, b):
    return jnp.dot(a, b, preferred_element_type=F32)


def outer(a, b):
    return lax.dot_general(a, b, (((1,), (1,)), ((), ())), preferred_element_type=F32)


def damp(u, h):
    wide_h = h.astype(F32)
    return (u * (1.0 - wide_h * wide_h)).astype(BF16)


def span(i):
    return pl.ds(pl.multiple_of(i * CHUNK, CHUNK), CHUNK)


def padded_rows(src, tall, flat, flipped):
    tall[...] = jnp.zeros(tall.shape, F32)
    tall[:Q] = src[...].astype(F32)
    flat[...] = tall[...].astype(BF16)
    flipped[...] = tall[...].T.astype(BF16)


BIG = 2
STAGES = 6
DIRECT = True


class Total:
    def __init__(self, blocks, slabs, hid, grads, out, land_c, half, land_a, land_all, tile, land_z, sems, scale):
        self.me, self.level = lax.axis_index("blocks"), lax.axis_index("slab")
        self.chips, self.slabs, self.pairs, self.scale = blocks // 2, slabs, slabs // 2, scale
        self.core, self.chip = lax.rem(self.me, 2), self.me // 2
        self.low, self.high = lax.rem(self.level, 2), self.level // 2
        self.grads, self.out, self.land_c, self.half = grads, out, land_c, half
        self.land_a, self.land_all, self.tile, self.land_z, self.sems = land_a, land_all, tile, land_z, sems
        self.hid = hid
        self.rows = piece_rows(blocks, slabs, hid)
        self.first = [sum(2 * n for n in self.rows[:p]) for p in range(len(self.rows))]
        self.flying = [[] for _ in self.rows]
        self.done = []

    def go(self, p, src, dst, which, device):
        copy = pltpu.make_async_remote_copy(
            src_ref=src, dst_ref=dst, send_sem=self.sems.at[0, p, which], recv_sem=self.sems.at[1, p, which],
            device_id=device, device_id_type=MESH,
        )
        copy.start()
        self.flying[p].append(copy)
        self.done.append(copy)

    def settle(self, p):
        for copy in self.flying[p]:
            copy.wait_recv()
        self.flying[p] = []

    def rows_of(self, p, core):
        n = self.rows[p]
        return pl.ds(pl.multiple_of(self.first[p] + core * n, 8), n)

    def size(self, p):
        return part_size(self.rows[p], self.chips * self.spread(p), self.hid)

    def part(self, p, t, start):
        n, w = self.size(p)
        across = self.hid // w
        rows = pl.ds(pl.multiple_of(start + t // across * n, 8), n)
        return rows, pl.ds(pl.multiple_of(lax.rem(t, across) * w, 128), w)

    def twin(self):
        return {"blocks": self.me + 1 - 2 * self.core}

    def spread(self, p):
        return self.slabs if self.direct(p) else 2

    def direct(self, p):
        return DIRECT and p == BIG

    def at(self, p):
        return self.chip * self.spread(p) + (self.level if self.direct(p) else self.low)

    def near(self, p):
        spread, base = self.spread(p), 0 if self.direct(p) else self.high * 2
        count = self.chips * spread
        for d in range(1, count):
            t = lax.rem(self.at(p) + d, count)
            yield d - 1, t, {"blocks": t // spread * 2 + self.core, "slab": base + lax.rem(t, spread)}

    def far(self):
        for d in range(1, self.pairs):
            yield d - 1, {"slab": lax.rem(self.high + d, self.pairs) * 2 + self.low}

    def friends(self):
        return [device for _, _, device in self.near(BIG)] + ([] if DIRECT else [device for _, device in self.far()])

    def stage(self, p, number):
        n, w = self.size(p)
        whole, small = pl.ds(0, self.rows[p]), (pl.ds(0, n), pl.ds(0, w))
        land = self.land_all if p == BIG else self.land_a.at[p]
        count = self.chips * self.spread(p)
        again = count + self.pairs
        start = self.first[p] + self.core * self.rows[p]
        self.settle(p)

        def gathered():
            total = self.half[p, *self.part(p, self.at(p), 0)]
            for i in range(count - 1):
                total += land[i, *small]
            return total

        def hand_out(total):
            spot = self.out.at[*self.part(p, self.at(p), start)]
            spot[...] = total * self.scale
            for i, t, device in self.near(p):
                self.go(p, spot, spot, again + i, device)

        if number == 0:
            self.go(p, self.grads.at[self.rows_of(p, 1 - self.core)], self.land_c.at[p, whole], 0, self.twin())
        elif number == 1:
            self.half[p, whole] = self.grads[self.rows_of(p, self.core)] + self.land_c[p, whole]
            for i, t, device in self.near(p):
                self.go(p, self.half.at[p, *self.part(p, t, 0)], land.at[i, *small], 1 + i, device)
        elif number == 2 and self.direct(p):
            hand_out(gathered())
        elif number == 2:
            tile = self.tile.at[p, *small]
            tile[...] = gathered()
            for i, device in self.far():
                self.go(p, tile, self.land_z.at[p, i, *small], count + i, device)
        elif number == 3 and not self.direct(p):
            total = self.tile[p, *small]
            for i in range(self.pairs - 1):
                total += self.land_z[p, i, *small]
            hand_out(total)
        elif number == STAGES - 2 - self.direct(p):
            rows = self.out.at[self.rows_of(p, self.core)]
            self.go(p, rows, rows, again + count, self.twin())

    def close(self):
        for copy in self.done:
            copy.wait_send()


def piece_rows(blocks, slabs, hid):
    return [hid // BIG // 2] * BIG + [max(R + 8, blocks // 2 * slabs * 8 * LANES // hid)]


def part_size(rows, count, hid):
    n = max(rows // count, 8)
    return n, rows // n * hid // count


OFFSETS = [d for d in range(-REACH, REACH + 1) if d != 0]


class Exchange:
    def __init__(self, blocks, slabs):
        me, level = lax.axis_index("blocks"), lax.axis_index("slab")
        self.side = [lax.rem(me - d + blocks, blocks) for d in OFFSETS]
        self.other = me + 1 - 2 * lax.rem(me, 2)
        self.above, self.below = lax.rem(level + 1, slabs), lax.rem(level + slabs - 1, slabs)
        self.friends = []

    def greet(self):
        barrier = pltpu.get_barrier_semaphore()
        for target in self.side:
            pl.semaphore_signal(barrier, inc=1, device_id={"blocks": target}, device_id_type=MESH)
        for target in (self.above, self.below):
            pl.semaphore_signal(barrier, inc=1, device_id={"slab": target}, device_id_type=MESH)
        for device in self.friends:
            pl.semaphore_signal(barrier, inc=1, device_id=device, device_id_type=MESH)

    def meet(self):
        pl.semaphore_wait(pltpu.get_barrier_semaphore(), len(self.side) + 2 + len(self.friends))

    def send(self, sheets, recv, sems):
        plan = [(0, i, {"blocks": target}) for i, target in enumerate(self.side)]
        plan.append((1, 2 * REACH, {"blocks": self.other}))
        plan.append((2, 2 * REACH + 1, {"slab": self.below}))
        plan.append((2, 2 * REACH + 2, {"slab": self.above}))
        copies = []
        for which, slot, device in sorted(plan, key=lambda row: -row[0]):
            copy = pltpu.make_async_remote_copy(
                src_ref=sheets.at[which, pl.ds(0, SHEET)], dst_ref=recv.at[slot, pl.ds(0, SHEET)],
                send_sem=sems.at[0, slot], recv_sem=sems.at[1, slot],
                device_id=device, device_id_type=MESH,
            )
            copy.start()
            copies.append(copy)
        return copies


def arrive(copies):
    for copy in copies:
        copy.wait_recv()


def step_kernel(
    blocks, slabs, source, level, quadrant, pops_hbm, cot_hbm, w_in_hbm, w_mid_hbm, w_out_hbm,
    final, grad_pops, out,
    grads, land_c, half_c, land_a, land_all, tile, land_z, total_sems, fa, fb, ca, cb, x1, x2, e, e2, h0a, h1a, h0b, h1b, a1, a0, u,
    sheets0, sheets1, sheets2, sheets3, recv0, recv1, recv2, recv3, tmp, ghosts, shifted, picks, w_in, w_in_t, w_out, w_out_t, w_mid_t, tall,
    pops, cot, w_in_rows, w_mid, w_out_rows, load_sems, sems,
):
    loads = [
        pltpu.make_async_copy(src, dst, load_sems.at[i])
        for i, (src, dst) in enumerate(
            ((cot_hbm, cot), (pops_hbm, pops), (w_in_hbm, w_in_rows), (w_out_hbm, w_out_rows), (w_mid_hbm, w_mid))
        )
    ]
    for copy in loads:
        copy.start()
    g = Grid()
    cells = x1.shape[1]
    hid = w_mid.shape[0]
    chunks = cells // CHUNK
    for ref in (recv0, recv1, recv2, recv3):
        ref[:, SHEET:, :] = jnp.zeros((ref.shape[0], SHEET_ROWS - SHEET, LANES), F32)
    link = Exchange(blocks, slabs)
    total = Total(
        blocks, slabs, hid, grads, out, land_c, half_c, land_a, land_all, tile, land_z, total_sems,
        float(blocks * slabs * cells) ** (-0.5),
    )
    link.friends = total.friends()
    second = hid + total.rows[BIG]
    link.greet()
    slots = [slot_of(source, blocks, face) for face in (0, 1)]
    for ref in (fa, fb, cb):
        ref[Q * PITCH :, :] = jnp.zeros((ROWS - Q * PITCH, LANES), F32)
    tmp[...] = jnp.zeros(tmp.shape, F32)

    build_picks(level, quadrant, picks, True, (0, 1, 2))
    loads[0].wait()
    from_cells(ca, cot)
    send_bars(g, ca, tmp, sheets0, picks)
    link.meet()
    bars2 = link.send(sheets0, recv0, sems.at[0])

    for copy in loads[1:]:
        copy.wait()
    padded_rows(w_in_rows, tall, w_in_t, w_in)
    padded_rows(w_out_rows, tall, w_out, w_out_t)
    from_cells(fa, pops)

    def forward(f, x, h0, h1, lifted):
        @pl.loop(0, chunks)
        def _(i):
            at = span(i)
            state = get_lines(f, i)
            inputs = state.astype(BF16)
            x[:, at] = inputs
            first = jnp.tanh(mm(w_in[...], inputs)).astype(BF16)
            h0[:, at] = first
            second = jnp.tanh(mm(w_mid[...], first)).astype(BF16)
            h1[:, at] = second
            if lifted:
                a1[:, at] = damp(u[:, at], second)
            put_lines(f, i, state + mm(w_out[...], second))

    def backward(p, h0):
        @pl.loop(0, chunks)
        def _(i):
            at = span(i)
            first = damp(mm(w_mid_t[...], a1[:, at]), h0[:, at])
            a0[:, at] = first
            put_lines(p, i, get_lines(p, i) + mm(w_in_t[...], first))

    def lift(p):
        @pl.loop(0, chunks)
        def _(i):
            at = span(i)
            err = get_lines(p, i).astype(BF16)
            e2[:, at] = err
            u[:, at] = mm(w_out_t[...], err)

    def top_down(h1, first, count):
        rows = pl.ds(first, count)

        @pl.loop(0, chunks)
        def _(i):
            at = span(i)
            a1[rows, at] = damp(mm(w_out_t[rows], e[:, at]), h1[rows, at])

    def bottom(p, h0, i):
        at = pl.ds(i * CHUNK, CHUNK)
        first = damp(mm(w_mid_t[...], a1[:, at]), h0[:, at])
        a0[:, at] = first
        put_lines(p, i, get_lines(p, i) + mm(w_in_t[...], first))

    def weigh(first, left, right, old, columns=None):
        value = outer(left[...], right[...])
        spot_rows = pl.ds(first, value.shape[0])
        at = (spot_rows, columns or slice(None))
        grads[at] = grads[at] + value if old else value

    forward(fa, x1, h0a, h1a, False)
    gather_sheets(g, fa, sheets1)
    posts1 = link.send(sheets1, recv1, sems.at[1])
    w_mid_t[...] = w_mid[...].astype(F32).T.astype(BF16)
    build_picks(level, quadrant, picks, False, (1, 2))
    arrive(bars2)
    stream_back(g, ca, recv0, slots, functools.partial(save, cb))
    lift(cb)
    arrive(posts1)
    settle(recv1, slots, picks, fa, ghosts)
    stream(g, fa, ghosts, shifted, functools.partial(save, fb))

    forward(fb, x2, h0b, h1b, True)
    gather_sheets(g, fb, sheets2)
    posts2 = link.send(sheets2, recv2, sems.at[2])
    backward(cb, h0b)
    send_bars(g, cb, tmp, sheets3, picks)
    bars1 = link.send(sheets3, recv3, sems.at[3])
    mid = hid // 2
    grads[hid:] = jnp.zeros((grads.shape[0] - hid, hid), F32)
    weigh(0, a1.at[:mid], h0b, False)
    weigh(mid, a1.at[mid:], h0b, False)
    weigh(hid, x2, a0, False)
    arrive(posts2)
    settle(recv2, slots, picks, fb, ghosts)
    stream(g, fb, ghosts, shifted, functools.partial(to_cells, final))
    arrive(bars1)
    stream_back(g, cb, recv3, slots, functools.partial(save, fa))
    for i in range(chunks):
        e[:, i * CHUNK : (i + 1) * CHUNK] = get_lines(fa, i).astype(BF16)

    def turns(*pairs):
        pairs = pairs if isinstance(pairs[0], tuple) else (pairs,)
        for p, number in pairs:
            total.stage(p, number)

    low, high = range(BIG // 2), range(BIG // 2, BIG)

    def turn(number, *groups):
        for group in groups:
            for p in group:
                total.stage(p, number)

    top_down(h1a, 0, mid)
    weigh(0, a1.at[:mid], h0a, True)
    turn(0, low)
    top_down(h1a, mid, mid)
    weigh(mid, a1.at[mid:], h0a.at[:mid], True, slice(0, mid))
    turn(1, low)
    weigh(mid, a1.at[mid:], h0a.at[mid:], True, slice(mid, hid))
    turn(0, high)
    weigh(second, e2, h1b, False)
    turn(1, high)
    weigh(second, e, h1a, True)
    for i in range(chunks):
        bottom(fa, h0a, i)
    turn(2, low)
    weigh(hid, x1, a0, True)
    turn(0, [BIG])
    turn(2, high)
    turn(1, [BIG])
    for q in range(Q):
        for half in range(HALVES):
            to_cells(grad_pops, q, half, load(fa, q, half))
    turn(3, low, high)
    turn(2, [BIG])
    turn(4, low)
    turn(3, [BIG])
    turn(4, high)
    turn(4, [BIG])
    turn(5, low, high, [BIG])
    total.close()
    for copies in (bars2, posts1, posts2, bars1):
        for copy in copies:
            copy.wait_send()


def leave_kernel(final, grad_pops, total, final_out, pops_out, mid_out, in_out, out_out, first_small, second_small, sems):
    hid = mid_out.shape[0]
    second = total.shape[0] - (total.shape[0] - hid) // 2
    first_small[...] = total[hid : hid + Q, :]
    second_small[...] = total[second : second + Q, :]
    plan = [
        (total.at[pl.ds(0, hid)], mid_out),
        (final, final_out),
        (grad_pops, pops_out),
        (first_small, in_out),
        (second_small, out_out),
    ]
    copies = [pltpu.make_async_copy(src, dst, sems.at[i]) for i, (src, dst) in enumerate(plan)]
    for copy in copies:
        copy.start()
    for copy in copies:
        copy.wait()


def vmem(count):
    return [pl.BlockSpec(memory_space=pltpu.VMEM)] * count


SMEM_SPEC = pl.BlockSpec(memory_space=pltpu.SMEM)
LIMIT = 50 * 1024 * 1024


def shape(dims, dtype=F32):
    return jax.ShapeDtypeStruct(dims, dtype)


def shards(blocks, slabs, populations, w_in, w_mid, w_out, cotangent, face_source, face_level, face_quadrant):
    cells = populations.shape[-1]
    hid = w_in.shape[0]
    pops, cot = (v.reshape(Q * cells // LANES, LANES) for v in (populations, cotangent))
    w_mid = w_mid[0]
    pieces = piece_rows(blocks, slabs, hid)
    rows, most = 2 * sum(pieces), max(pieces)
    small, last = part_size(pieces[0], blocks, hid), part_size(pieces[-1], blocks // 2 * (slabs if DIRECT else 2), hid)
    pieces = len(pieces)
    volume = pltpu.VMEM((ROWS, LANES), F32)
    thin = pltpu.VMEM((R, cells), BF16)
    deep = pltpu.VMEM((hid, cells), BF16)
    slots = 2 * REACH + 3
    final, grad_pops, total = pl.pallas_call(
        functools.partial(step_kernel, blocks, slabs),
        out_shape=(shape(pops.shape), shape(pops.shape), shape((rows, hid))),
        in_specs=[SMEM_SPEC] * 3 + [pl.BlockSpec(memory_space=pltpu.HBM)] * 5,
        out_specs=tuple(vmem(3)),
        scratch_shapes=[
            pltpu.VMEM((rows, hid), F32),
            pltpu.VMEM((pieces, most, hid), F32),
            pltpu.VMEM((pieces, most, hid), F32),
            pltpu.VMEM((BIG, blocks - 1, *small), F32),
            pltpu.VMEM((blocks // 2 * (slabs if DIRECT else 2) - 1, *last), F32),
            pltpu.VMEM((pieces, *small), F32),
            pltpu.VMEM((pieces, max(slabs // 2 - 1, 1), *small), F32),
            pltpu.SemaphoreType.DMA((2, pieces, blocks * slabs + slabs // 2 + 1)),
        ] + [volume] * 4 + [thin] * 4 + [deep] * 6 + [pltpu.VMEM((hid, cells), F32)] + [
            *[pltpu.VMEM((3, SHEET_ROWS, LANES), F32)] * 4,
            *[pltpu.VMEM((slots, SHEET_ROWS, LANES), F32)] * 4,
            pltpu.VMEM((3, SHEET_ROWS, LANES), F32),
            pltpu.VMEM((4 * HALVES * 8, LANES), F32),
            pltpu.VMEM((16 * BLOCK, LANES), F32),
            pltpu.VMEM((10, A, A), BF16),
            pltpu.VMEM((hid, R), BF16),
            pltpu.VMEM((R, hid), BF16),
            pltpu.VMEM((R, hid), BF16),
            pltpu.VMEM((hid, R), BF16),
            pltpu.VMEM((hid, hid), BF16),
            pltpu.VMEM((R, hid), F32),
            pltpu.VMEM(pops.shape, F32),
            pltpu.VMEM(cot.shape, F32),
            pltpu.VMEM((Q, hid), BF16),
            pltpu.VMEM((hid, hid), BF16),
            pltpu.VMEM((Q, hid), BF16),
            pltpu.SemaphoreType.DMA((5,)),
            pltpu.SemaphoreType.DMA((4, 2, slots)),
        ],
        compiler_params=pltpu.CompilerParams(vmem_limit_bytes=LIMIT, collective_id=0, has_side_effects=True),
        name="step",
    )(*[
        pltpu.with_memory_space_constraint(v, pltpu.HBM)
        for v in (face_source.T, face_level, face_quadrant, pops, cot, w_in.T, w_mid, w_out)
    ])
    final, grad_pops, grad_mid, grad_in, grad_out = pl.pallas_call(
        leave_kernel,
        out_shape=(
            shape(pops.shape), shape(pops.shape), shape((hid, hid)), shape((Q, hid)), shape((Q, hid)),
        ),
        in_specs=vmem(3),
        out_specs=tuple([pl.BlockSpec(memory_space=pl.ANY)] * 5),
        scratch_shapes=[pltpu.VMEM((Q, hid), F32), pltpu.VMEM((Q, hid), F32), pltpu.SemaphoreType.DMA((5,))],
        compiler_params=pltpu.CompilerParams(vmem_limit_bytes=4 * 1024 * 1024),
        name="leave",
    )(final, grad_pops, total)
    return (
        final.reshape(populations.shape),
        grad_pops.reshape(populations.shape),
        grad_in.T,
        grad_mid[None],
        grad_out,
    )


def solution(mesh):
    spread = P(None, "slab", "blocks", None)
    in_specs = (spread, P(), P(), P(), spread, P(), P("slab", "blocks", None), P("slab", "blocks", None))
    out_specs = (spread, spread, P(), P(), P())
    body = functools.partial(shards, mesh.shape["blocks"], mesh.shape["slab"])
    return jax.shard_map(body, mesh=mesh, in_specs=in_specs, out_specs=out_specs, check_vma=False)
```

```python
import functools

import jax
import jax.numpy as jnp
from jax import lax
from jax.experimental import pallas as pl
from jax.experimental.pallas import tpu as pltpu
from jax.sharding import PartitionSpec as P

REACH = 3
R = 24
S = 16
A = S * S
LANES = 128
HALVES = A // LANES
CHUNK = 1024
LINES = CHUNK // LANES
BLOCK = S + 2
PITCH = HALVES * BLOCK
ROWS = R * PITCH
MESH = pl.DeviceIdType.MESH
F32, BF16 = jnp.float32, jnp.bfloat16

VELOCITIES = [
    (0, 0, 0),
    (1, 0, 0),
    (-1, 0, 0),
    (0, 1, 0),
    (0, -1, 0),
    (0, 0, 1),
    (0, 0, -1),
    (1, 1, 0),
    (-1, -1, 0),
    (1, -1, 0),
    (-1, 1, 0),
    (1, 0, 1),
    (-1, 0, -1),
    (1, 0, -1),
    (-1, 0, 1),
    (0, 1, 1),
    (0, -1, -1),
    (0, 1, -1),
    (0, -1, 1),
]
Q = len(VELOCITIES)
OPPOSITE = [VELOCITIES.index((-a, -b, -c)) for a, b, c in VELOCITIES]
FACED = 5
SHEET = 2 * HALVES * FACED
SHEET_ROWS = 24


def members(axis, side):
    return [q for q, v in enumerate(VELOCITIES) if v[axis] == (1, -1)[side]]


def place(q, axis):
    side = 0 if VELOCITIES[q][axis] == 1 else 1
    return side, members(axis, side).index(q)


def base(q, half):
    return q * PITCH + half * BLOCK + 1


def load(ref, q, half, off=0):
    return ref[pl.ds(base(q, half) + off, S), :]


def save(ref, q, half, value):
    ref[pl.ds(base(q, half), S), :] = value


def get_lines(ref, i):
    first = i * (LINES // HALVES)
    return jnp.concatenate(
        [ref[pl.ds(j % HALVES * BLOCK + 1 + j // HALVES + first, R, stride=PITCH), :] for j in range(LINES)], axis=1
    )


def put_lines(ref, i, value):
    first = i * (LINES // HALVES)
    for j in range(LINES):
        at = pl.ds(j % HALVES * BLOCK + 1 + j // HALVES + first, R, stride=PITCH)
        ref[at, :] = value[:, j * LANES : (j + 1) * LANES]


def from_cells(dst, src):
    for q in range(Q):
        for half in range(HALVES):
            save(dst, q, half, src[pl.ds(q * S * HALVES + half, S, stride=HALVES), :])


def to_cells(dst, q, half, value):
    dst[pl.ds(q * S * HALVES + half, S, stride=HALVES), :] = value


class Grid:
    def __init__(self):
        self.x = lax.broadcasted_iota(jnp.int32, (S, LANES), 0)
        self.lane = lax.broadcasted_iota(jnp.int32, (S, LANES), 1)
        self.y = self.lane // S
        self.z = self.lane % S
        self.lane1 = lax.broadcasted_iota(jnp.int32, (1, LANES), 1)
        self.y1, self.z1 = self.lane1 // S, self.lane1 % S


def roll(x, shift):
    shift %= LANES
    return x if shift == 0 else pltpu.roll(x, shift, 1)


def fan(x, shift, stride):
    return pltpu.roll(x, shift % LANES, 1, stride=stride, stride_axis=0)


def carry(g, pair, step, lane):
    if step == 1:
        return [pair[0], jnp.where(lane < LANES - S, pair[1], pair[0])]
    if step == -1:
        return [jnp.where(lane >= S, pair[0], pair[1]), pair[1]]
    return pair


def wide(row):
    return jnp.broadcast_to(row, (8, LANES))


def spread_y(row_of, side):
    shift = 0 if side == 0 else -(LANES - S)
    return jnp.concatenate([fan(wide(row_of(half)), shift, S) for half in range(HALVES)], axis=0)


def spread_z(g, row_of, z, dy):
    pair = carry(g, [row_of(half) for half in range(HALVES)], dy, g.lane1)
    return [
        jnp.concatenate([fan(wide(row), z - (S - 1) + S * dy + 8 * part, 1) for part in range(2)], axis=0) for row in pair
    ]


def total_rows(x):
    return jnp.sum(x, axis=0, keepdims=True)


def sheet_row(side, half, r):
    return (side * HALVES + half) * FACED + r


def put_row(ref, side, half, r, value):
    at = sheet_row(side, half, r)
    ref[at : at + 1, :] = value


def fold_y(x, high):
    shift = S if high else 0
    return [total_rows(fan(x[8 * part : 8 * part + 8], shift, S)) for part in range(2)]


def fold_z(x, z):
    return total_rows(sum(fan(x[8 * part : 8 * part + 8], 8 * part - z, 1) for part in range(2)))


def gather_sheets(g, post, sheets):
    for q, v in enumerate(VELOCITIES):
        if v[0]:
            side, r = place(q, 0)
            for half in range(HALVES):
                at = base(q, half) + (S - 1 if v[0] == 1 else 0)
                put_row(sheets.at[0], side, half, r, post[at : at + 1, :])
        if v[1]:
            side, r = place(q, 1)
            high = v[1] == 1
            x = jnp.where(g.y == (7 if high else 0), load(post, q, 1 if high else 0), 0.0)
            for part, row in enumerate(fold_y(x, high)):
                put_row(sheets.at[1], side, part, r, row)
        if v[2]:
            side, r = place(q, 2)
            z = S - 1 if v[2] == 1 else 0
            for half in range(HALVES):
                row = fold_z(jnp.where(g.z == z, load(post, q, half), 0.0), z)
                put_row(sheets.at[2], side, half, r, row)


def inside_z(z, dz):
    return z != (0 if dz == 1 else S - 1)


def gather_bars(g, bar, tmp):
    last = LANES // S - 1
    for q, (dx, dy, dz) in enumerate(VELOCITIES):
        if dx:
            side, r = place(q, 0)
            rows = []
            for half in range(HALVES):
                at = base(q, half) + (0 if dx == 1 else S - 1)
                row = bar[at : at + 1, :]
                rows.append(jnp.where(inside_z(g.z1, dz), row, 0.0) if dz else row)
            rows = [roll(row, -S * dy - dz) for row in carry(g, rows, -dy, g.lane1)]
            if dy:
                half, y = (1, last) if dy == 1 else (0, 0)
                rows[half] = jnp.where(g.y1 == y, 0.0, rows[half])
            for half in range(HALVES):
                put_row(tmp.at[0], side, half, r, rows[half])
        if dy:
            side, r = place(q, 1)
            keep = g.y == (0 if dy == 1 else last)
            if dz:
                keep &= inside_z(g.z, dz)
            if dx:
                keep &= g.x != (S - 1 if dx == 1 else 0)
            x = jnp.where(keep, load(bar, q, 0 if dy == 1 else 1, dx), 0.0)
            for part, row in enumerate(fold_y(x, dy == -1)):
                put_row(tmp.at[1], side, part, r, roll(row, -dz))
        if dz:
            side, r = place(q, 2)
            z = 0 if dz == 1 else S - 1
            rows = []
            for half in range(HALVES):
                keep = g.z == z
                if dx:
                    keep &= g.x != (S - 1 if dx == 1 else 0)
                if dy and half == (0 if dy == 1 else 1):
                    keep &= g.y != (0 if dy == 1 else last)
                rows.append(fold_z(jnp.where(keep, load(bar, q, half, dx), 0.0), z))
            rows = [roll(row, -S * dy) for row in carry(g, rows, -dy, g.lane1)]
            if dy:
                half, y = (1, last) if dy == 1 else (0, 0)
                rows[half] = jnp.where(g.y1 == y, 0.0, rows[half])
            for half in range(HALVES):
                put_row(tmp.at[2], side, half, r, rows[half])


def refined(halves, pick, transposed):
    sheet = jnp.concatenate(halves, axis=1)
    hi = sheet.astype(BF16).astype(F32)
    rest = sheet - hi
    mid = rest.astype(BF16).astype(F32)
    parts = jnp.concatenate([hi, mid, rest - mid], axis=0).astype(BF16)
    dims = (((1,), (1 if transposed else 0,)), ((), ()))
    r = lax.dot_general(parts, pick, dims, preferred_element_type=F32)
    return r[:8] + r[8:16] + r[16:]


def sheet_halves(ref, side):
    return [ref[pl.ds(sheet_row(side, half, 0), 8), :] for half in range(HALVES)]


def send_bars(g, bar, tmp, sheets, picks):
    gather_bars(g, bar, tmp)
    for axis in range(3):
        for side in range(2):
            out = refined(sheet_halves(tmp.at[axis], side), picks[pick_at(axis, side, True)], True)
            for half in range(HALVES):
                sheets[axis, pl.ds(sheet_row(side, half, 0), FACED), :] = out[:FACED, half * LANES : (half + 1) * LANES]


def pick_at(axis, side, back):
    if axis == 0:
        return side
    return 2 + 8 // 2 * back + 2 * (axis - 1) + side


def build_picks(level, quadrant, picks, back, axes):
    lane = lax.broadcasted_iota(jnp.int32, (1, A), 1)
    source = lax.broadcasted_iota(jnp.int32, (A, A), 0)
    half = S // 2

    def turned(axis, i):
        if axis == 0:
            return i
        if axis == 1:
            return i // LANES * LANES + (7 - i // S % 8) * S + i % S
        return i // S * S + (S - 1 - i % S)

    for axis in axes:
        for side in range(2):
            face = 2 * axis + 1 - side
            quad = quadrant[0, 0, face]
            first, second = quad // 2, quad % 2
            if axis == 2:
                first, second = second, first

            def wanted(i):
                fine = (first * half + i // S // 2) * S + second * half + i % S // 2
                return jnp.where(level[0, 0, face] == 1, fine, i)

            want = turned(axis, wanted(lane)) if back else wanted(turned(axis, lane))
            picks[pick_at(axis, side, back)] = jnp.where(source == want, 1.0, 0.0).astype(BF16)


def slot_of(source, blocks, face):
    me = lax.axis_index("blocks")
    distance = lax.rem(source[face, me] - me + blocks, blocks)
    distance = jnp.where(distance > blocks // 2, distance - blocks, distance)
    slot = jnp.where(distance < 0, distance + REACH, distance + REACH - 1)
    return jnp.clip(slot, 0, 2 * REACH - 1)


def ghost_row(axis, side, half, r):
    return (((axis - 1) * 2 + side) * HALVES + half) * 8 + r


def settle(recv, slots, picks, post, ghosts):
    for side in range(2):
        slot = slots[1 - side]
        halves = [recv[slot, pl.ds(sheet_row(side, half, 0), 8), :] for half in range(HALVES)]
        out = refined(halves, picks[pick_at(0, side, False)], False)
        for r, q in enumerate(members(0, side)):
            for half in range(HALVES):
                at = base(q, half) + (-1 if side == 0 else S)
                post[at : at + 1, :] = out[r : r + 1, half * LANES : (half + 1) * LANES]
    for axis in (1, 2):
        for side in range(2):
            slot = 2 * REACH if axis == 1 else 2 * REACH + (2 if side == 0 else 1)
            out = refined(sheet_halves(recv.at[slot], side), picks[pick_at(axis, side, False)], False)
            for half in range(HALVES):
                at = ghost_row(axis, side, half, 0)
                ghosts[at : at + 8, :] = out[:, half * LANES : (half + 1) * LANES]


def stream(g, post, ghosts, shifted, store):
    last = LANES // S - 1
    used = [0]

    def moved(value, dx):
        if not dx:
            return value
        at = used[0] * BLOCK + 1
        used[0] += 1
        shifted[pl.ds(at, S), :] = value
        return shifted[pl.ds(at - dx, S), :]

    for q, (dx, dy, dz) in enumerate(VELOCITIES):
        t = [load(post, q, half, -dx) for half in range(HALVES)]
        if dy:
            side, r = place(q, 1)

            def row_y(half):
                at = ghost_row(1, side, half, r)
                return ghosts[at : at + 1, :]

            halo = moved(spread_y(row_y, side), dx)
            if dy == 1:
                inner = g.lane < LANES - S
                t = [jnp.where(inner, t[0], halo), jnp.where(inner, t[1], t[0])]
            else:
                inner = g.lane >= S
                t = [jnp.where(inner, t[0], t[1]), jnp.where(inner, t[1], halo)]
        t = [roll(x, S * dy + dz) for x in t]
        if dz:
            side, r = place(q, 2)
            z = 0 if dz == 1 else S - 1

            def row_z(half):
                at = ghost_row(2, side, half, r)
                return ghosts[at : at + 1, :]

            halo = [moved(x, dx) for x in spread_z(g, row_z, z, dy)]
            t = [jnp.where(g.z == z, halo[half], t[half]) for half in range(HALVES)]
        for half in range(HALVES):
            two = crossed(g, half, dx, dy, dz)
            if two is not None:
                t[half] = jnp.where(two, load(post, OPPOSITE[q], half), t[half])
            store(q, half, t[half])


def crossed(g, half, dx, dy, dz):
    if (dx != 0) + (dy != 0) + (dz != 0) < 2:
        return None
    if dy and half != (0 if dy == 1 else 1):
        return None
    on = None
    for d, c, top in ((dx, g.x, S - 1), (dy, g.y, LANES // S - 1), (dz, g.z, S - 1)):
        if d:
            hit = c == (0 if d == 1 else top)
            on = hit if on is None else on & hit
    return on


def stream_back(g, bar, recv, slots, store):
    last = LANES // S - 1
    for q, (dx, dy, dz) in enumerate(VELOCITIES):
        t = [load(bar, q, half, dx) for half in range(HALVES)]
        t = [roll(x, -S * dy - dz) for x in carry(g, t, -dy, g.lane)]
        faces = []
        if dx:
            side, r = place(q, 0)
            slot = slots[side]
            rows = [recv[slot, pl.ds(sheet_row(side, half, r), 1), :] for half in range(HALVES)]
            rows = [jnp.broadcast_to(row, (S, LANES)) for row in rows]
            faces.append((rows, [g.x == (S - 1 if dx == 1 else 0)] * 2))
        if dy:
            side, r = place(q, 1)
            full = spread_y(lambda half: recv[2 * REACH, pl.ds(sheet_row(side, half, r), 1), :], side)
            mask = g.y == (last if dy == 1 else 0)
            faces.append(([full, full], [mask if half == (1 if dy == 1 else 0) else None for half in range(HALVES)]))
        if dz:
            side, r = place(q, 2)
            slot = 2 * REACH + (1 if side == 0 else 2)
            z = S - 1 if dz == 1 else 0
            full = spread_z(g, lambda half: recv[slot, pl.ds(sheet_row(side, half, r), 1), :], z, 0)
            faces.append((full, [g.z == z] * 2))
        for half in range(HALVES):
            here = [(value[half], mask[half]) for value, mask in faces if mask[half] is not None]
            out = t[half]
            if len(here) == 1:
                out = jnp.where(here[0][1], here[0][0], out)
            if len(here) == 2:
                (va, ma), (vb, mb) = here
                both = va + vb + load(bar, OPPOSITE[q], half)
                out = jnp.where(mb, jnp.where(ma, both, vb), jnp.where(ma, va, out))
            store(q, half, out)


def mm(a, b):
    return jnp.dot(a, b, preferred_element_type=F32)


def outer(a, b):
    return lax.dot_general(a, b, (((1,), (1,)), ((), ())), preferred_element_type=F32)


def damp(u, h):
    wide_h = h.astype(F32)
    return (u * (1.0 - wide_h * wide_h)).astype(BF16)


def span(i):
    return pl.ds(pl.multiple_of(i * CHUNK, CHUNK), CHUNK)


def padded_rows(src, tall, flat, flipped):
    tall[...] = jnp.zeros(tall.shape, F32)
    tall[:Q] = src[...].astype(F32)
    flat[...] = tall[...].astype(BF16)
    flipped[...] = tall[...].T.astype(BF16)


BIG = 2
STAGES = 6
DIRECT = True


class Total:
    def __init__(self, blocks, slabs, hid, grads, out, land_c, half, land_a, land_all, tile, land_z, sems, scale):
        self.me, self.level = lax.axis_index("blocks"), lax.axis_index("slab")
        self.chips, self.slabs, self.pairs, self.scale = blocks // 2, slabs, slabs // 2, scale
        self.core, self.chip = lax.rem(self.me, 2), self.me // 2
        self.low, self.high = lax.rem(self.level, 2), self.level // 2
        self.grads, self.out, self.land_c, self.half = grads, out, land_c, half
        self.land_a, self.land_all, self.tile, self.land_z, self.sems = land_a, land_all, tile, land_z, sems
        self.hid = hid
        self.rows = piece_rows(blocks, slabs, hid)
        self.first = [sum(2 * n for n in self.rows[:p]) for p in range(len(self.rows))]
        self.flying = [[] for _ in self.rows]
        self.done = []

    def go(self, p, src, dst, which, device):
        copy = pltpu.make_async_remote_copy(
            src_ref=src, dst_ref=dst, send_sem=self.sems.at[0, p, which], recv_sem=self.sems.at[1, p, which],
            device_id=device, device_id_type=MESH,
        )
        copy.start()
        self.flying[p].append(copy)
        self.done.append(copy)

    def settle(self, p):
        for copy in self.flying[p]:
            copy.wait_recv()
        self.flying[p] = []

    def rows_of(self, p, core):
        n = self.rows[p]
        return pl.ds(pl.multiple_of(self.first[p] + core * n, 8), n)

    def size(self, p):
        return part_size(self.rows[p], self.chips * self.spread(p), self.hid)

    def part(self, p, t, start):
        n, w = self.size(p)
        across = self.hid // w
        rows = pl.ds(pl.multiple_of(start + t // across * n, 8), n)
        return rows, pl.ds(pl.multiple_of(lax.rem(t, across) * w, 128), w)

    def twin(self):
        return {"blocks": self.me + 1 - 2 * self.core}

    def spread(self, p):
        return self.slabs if self.direct(p) else 2

    def direct(self, p):
        return DIRECT and p == BIG

    def at(self, p):
        return self.chip * self.spread(p) + (self.level if self.direct(p) else self.low)

    def near(self, p):
        spread, base = self.spread(p), 0 if self.direct(p) else self.high * 2
        count = self.chips * spread
        for d in range(1, count):
            t = lax.rem(self.at(p) + d, count)
            yield d - 1, t, {"blocks": t // spread * 2 + self.core, "slab": base + lax.rem(t, spread)}

    def far(self):
        for d in range(1, self.pairs):
            yield d - 1, {"slab": lax.rem(self.high + d, self.pairs) * 2 + self.low}

    def friends(self):
        return [device for _, _, device in self.near(BIG)] + ([] if DIRECT else [device for _, device in self.far()])

    def stage(self, p, number):
        n, w = self.size(p)
        whole, small = pl.ds(0, self.rows[p]), (pl.ds(0, n), pl.ds(0, w))
        land = self.land_all if p == BIG else self.land_a.at[p]
        count = self.chips * self.spread(p)
        again = count + self.pairs
        start = self.first[p] + self.core * self.rows[p]
        self.settle(p)

        def gathered():
            total = self.half[p, *self.part(p, self.at(p), 0)]
            for i in range(count - 1):
                total += land[i, *small]
            return total

        def hand_out(total):
            spot = self.out.at[*self.part(p, self.at(p), start)]
            spot[...] = total * self.scale
            for i, t, device in self.near(p):
                self.go(p, spot, spot, again + i, device)

        if number == 0:
            self.go(p, self.grads.at[self.rows_of(p, 1 - self.core)], self.land_c.at[p, whole], 0, self.twin())
        elif number == 1:
            self.half[p, whole] = self.grads[self.rows_of(p, self.core)] + self.land_c[p, whole]
            for i, t, device in self.near(p):
                self.go(p, self.half.at[p, *self.part(p, t, 0)], land.at[i, *small], 1 + i, device)
        elif number == 2 and self.direct(p):
            hand_out(gathered())
        elif number == 2:
            tile = self.tile.at[p, *small]
            tile[...] = gathered()
            for i, device in self.far():
                self.go(p, tile, self.land_z.at[p, i, *small], count + i, device)
        elif number == 3 and not self.direct(p):
            total = self.tile[p, *small]
            for i in range(self.pairs - 1):
                total += self.land_z[p, i, *small]
            hand_out(total)
        elif number == STAGES - 2 - self.direct(p):
            rows = self.out.at[self.rows_of(p, self.core)]
            self.go(p, rows, rows, again + count, self.twin())

    def close(self):
        for copy in self.done:
            copy.wait_send()


def piece_rows(blocks, slabs, hid):
    return [hid // BIG // 2] * BIG + [max(R + 8, blocks // 2 * slabs * 8 * LANES // hid)]


def part_size(rows, count, hid):
    n = max(rows // count, 8)
    return n, rows // n * hid // count


OFFSETS = [d for d in range(-REACH, REACH + 1) if d != 0]


class Exchange:
    def __init__(self, blocks, slabs):
        me, level = lax.axis_index("blocks"), lax.axis_index("slab")
        self.side = [lax.rem(me - d + blocks, blocks) for d in OFFSETS]
        self.other = me + 1 - 2 * lax.rem(me, 2)
        self.above, self.below = lax.rem(level + 1, slabs), lax.rem(level + slabs - 1, slabs)
        self.friends = []

    def greet(self):
        barrier = pltpu.get_barrier_semaphore()
        for target in self.side:
            pl.semaphore_signal(barrier, inc=1, device_id={"blocks": target}, device_id_type=MESH)
        for target in (self.above, self.below):
            pl.semaphore_signal(barrier, inc=1, device_id={"slab": target}, device_id_type=MESH)
        for device in self.friends:
            pl.semaphore_signal(barrier, inc=1, device_id=device, device_id_type=MESH)

    def meet(self):
        pl.semaphore_wait(pltpu.get_barrier_semaphore(), len(self.side) + 2 + len(self.friends))

    def send(self, sheets, recv, sems):
        plan = [(0, i, {"blocks": target}) for i, target in enumerate(self.side)]
        plan.append((1, 2 * REACH, {"blocks": self.other}))
        plan.append((2, 2 * REACH + 1, {"slab": self.below}))
        plan.append((2, 2 * REACH + 2, {"slab": self.above}))
        copies = []
        for which, slot, device in sorted(plan, key=lambda row: -row[0]):
            copy = pltpu.make_async_remote_copy(
                src_ref=sheets.at[which, pl.ds(0, SHEET)], dst_ref=recv.at[slot, pl.ds(0, SHEET)],
                send_sem=sems.at[0, slot], recv_sem=sems.at[1, slot],
                device_id=device, device_id_type=MESH,
            )
            copy.start()
            copies.append(copy)
        return copies


def arrive(copies):
    for copy in copies:
        copy.wait_recv()


def step_kernel(
    blocks, slabs, source, level, quadrant, pops_hbm, cot_hbm, w_in_hbm, w_mid_hbm, w_out_hbm,
    final, grad_pops, out,
    grads, land_c, half_c, land_a, land_all, tile, land_z, total_sems, fa, fb, ca, cb, x1, x2, e, e2, h0a, h1a, h0b, h1b, a1, a0, u,
    sheets0, sheets1, sheets2, sheets3, recv0, recv1, recv2, recv3, tmp, ghosts, shifted, picks, w_in, w_in_t, w_out, w_out_t, w_mid_t, tall,
    pops, cot, w_in_rows, w_mid, w_out_rows, load_sems, sems,
):
    loads = [
        pltpu.make_async_copy(src, dst, load_sems.at[i])
        for i, (src, dst) in enumerate(
            ((cot_hbm, cot), (pops_hbm, pops), (w_in_hbm, w_in_rows), (w_out_hbm, w_out_rows), (w_mid_hbm, w_mid))
        )
    ]
    for copy in loads:
        copy.start()
    g = Grid()
    cells = x1.shape[1]
    hid = w_mid.shape[0]
    chunks = cells // CHUNK
    for ref in (recv0, recv1, recv2, recv3):
        ref[:, SHEET:, :] = jnp.zeros((ref.shape[0], SHEET_ROWS - SHEET, LANES), F32)
    link = Exchange(blocks, slabs)
    total = Total(
        blocks, slabs, hid, grads, out, land_c, half_c, land_a, land_all, tile, land_z, total_sems,
        float(blocks * slabs * cells) ** (-0.5),
    )
    link.friends = total.friends()
    second = hid + total.rows[BIG]
    link.greet()
    slots = [slot_of(source, blocks, face) for face in (0, 1)]
    for ref in (fa, fb, cb):
        ref[Q * PITCH :, :] = jnp.zeros((ROWS - Q * PITCH, LANES), F32)
    tmp[...] = jnp.zeros(tmp.shape, F32)

    build_picks(level, quadrant, picks, True, (0, 1, 2))
    loads[0].wait()
    from_cells(ca, cot)
    send_bars(g, ca, tmp, sheets0, picks)
    link.meet()
    bars2 = link.send(sheets0, recv0, sems.at[0])

    for copy in loads[1:]:
        copy.wait()
    padded_rows(w_in_rows, tall, w_in_t, w_in)
    padded_rows(w_out_rows, tall, w_out, w_out_t)
    from_cells(fa, pops)

    def forward(f, x, h0, h1, lifted):
        @pl.loop(0, chunks)
        def _(i):
            at = span(i)
            state = get_lines(f, i)
            inputs = state.astype(BF16)
            x[:, at] = inputs
            first = jnp.tanh(mm(w_in[...], inputs)).astype(BF16)
            h0[:, at] = first
            second = jnp.tanh(mm(w_mid[...], first)).astype(BF16)
            h1[:, at] = second
            if lifted:
                a1[:, at] = damp(u[:, at], second)
            put_lines(f, i, state + mm(w_out[...], second))

    def backward(p, h0):
        for i in range(chunks):
            at = pl.ds(i * CHUNK, CHUNK)
            first = damp(mm(w_mid_t[...], a1[:, at]), h0[:, at])
            a0[:, at] = first
            put_lines(p, i, get_lines(p, i) + mm(w_in_t[...], first))

    def lift(p):
        for i in range(chunks):
            at = pl.ds(i * CHUNK, CHUNK)
            err = get_lines(p, i).astype(BF16)
            e2[:, at] = err
            u[:, at] = mm(w_out_t[...], err)

    def top_down(h1, first, count):
        rows = pl.ds(first, count)

        for i in range(chunks):
            at = pl.ds(i * CHUNK, CHUNK)
            a1[rows, at] = damp(mm(w_out_t[rows], e[:, at]), h1[rows, at])

    def bottom(p, h0, i):
        at = pl.ds(i * CHUNK, CHUNK)
        first = damp(mm(w_mid_t[...], a1[:, at]), h0[:, at])
        a0[:, at] = first
        put_lines(p, i, get_lines(p, i) + mm(w_in_t[...], first))

    def weigh(first, left, right, old, columns=None):
        value = outer(left[...], right[...])
        spot_rows = pl.ds(first, value.shape[0])
        at = (spot_rows, columns or slice(None))
        grads[at] = grads[at] + value if old else value

    forward(fa, x1, h0a, h1a, False)
    gather_sheets(g, fa, sheets1)
    posts1 = link.send(sheets1, recv1, sems.at[1])
    w_mid_t[...] = w_mid[...].astype(F32).T.astype(BF16)
    build_picks(level, quadrant, picks, False, (1, 2))
    arrive(bars2)
    stream_back(g, ca, recv0, slots, functools.partial(save, cb))
    lift(cb)
    arrive(posts1)
    settle(recv1, slots, picks, fa, ghosts)
    stream(g, fa, ghosts, shifted, functools.partial(save, fb))

    forward(fb, x2, h0b, h1b, True)
    gather_sheets(g, fb, sheets2)
    posts2 = link.send(sheets2, recv2, sems.at[2])
    backward(cb, h0b)
    send_bars(g, cb, tmp, sheets3, picks)
    bars1 = link.send(sheets3, recv3, sems.at[3])
    mid = hid // 2
    grads[hid:] = jnp.zeros((grads.shape[0] - hid, hid), F32)
    weigh(0, a1.at[:mid], h0b, False)
    weigh(mid, a1.at[mid:], h0b, False)
    weigh(hid, x2, a0, False)
    arrive(posts2)
    settle(recv2, slots, picks, fb, ghosts)
    stream(g, fb, ghosts, shifted, functools.partial(to_cells, final))
    arrive(bars1)
    stream_back(g, cb, recv3, slots, functools.partial(save, fa))
    for i in range(chunks):
        e[:, i * CHUNK : (i + 1) * CHUNK] = get_lines(fa, i).astype(BF16)

    def turns(*pairs):
        pairs = pairs if isinstance(pairs[0], tuple) else (pairs,)
        for p, number in pairs:
            total.stage(p, number)

    low, high = range(BIG // 2), range(BIG // 2, BIG)

    def turn(number, *groups):
        for group in groups:
            for p in group:
                total.stage(p, number)

    top_down(h1a, 0, mid)
    weigh(0, a1.at[:mid], h0a, True)
    turn(0, low)
    top_down(h1a, mid, mid)
    weigh(mid, a1.at[mid:], h0a.at[:mid], True, slice(0, mid))
    turn(1, low)
    weigh(mid, a1.at[mid:], h0a.at[mid:], True, slice(mid, hid))
    turn(0, high)
    weigh(second, e2, h1b, False)
    turn(1, high)
    weigh(second, e, h1a, True)
    for i in range(chunks):
        bottom(fa, h0a, i)
    turn(2, low)
    weigh(hid, x1, a0, True)
    turn(0, [BIG])
    turn(2, high)
    turn(1, [BIG])
    for q in range(Q):
        for half in range(HALVES):
            to_cells(grad_pops, q, half, load(fa, q, half))
    turn(3, low, high)
    turn(2, [BIG])
    turn(4, low)
    turn(3, [BIG])
    turn(4, high)
    turn(4, [BIG])
    turn(5, low, high, [BIG])
    total.close()
    for copies in (bars2, posts1, posts2, bars1):
        for copy in copies:
            copy.wait_send()


def leave_kernel(final, grad_pops, total, final_out, pops_out, mid_out, in_out, out_out, first_small, second_small, sems):
    hid = mid_out.shape[0]
    second = total.shape[0] - (total.shape[0] - hid) // 2
    first_small[...] = total[hid : hid + Q, :]
    second_small[...] = total[second : second + Q, :]
    plan = [
        (total.at[pl.ds(0, hid)], mid_out),
        (final, final_out),
        (grad_pops, pops_out),
        (first_small, in_out),
        (second_small, out_out),
    ]
    copies = [pltpu.make_async_copy(src, dst, sems.at[i]) for i, (src, dst) in enumerate(plan)]
    for copy in copies:
        copy.start()
    for copy in copies:
        copy.wait()


def vmem(count):
    return [pl.BlockSpec(memory_space=pltpu.VMEM)] * count


SMEM_SPEC = pl.BlockSpec(memory_space=pltpu.SMEM)
LIMIT = 50 * 1024 * 1024


def shape(dims, dtype=F32):
    return jax.ShapeDtypeStruct(dims, dtype)


def shards(blocks, slabs, populations, w_in, w_mid, w_out, cotangent, face_source, face_level, face_quadrant):
    cells = populations.shape[-1]
    hid = w_in.shape[0]
    pops, cot = (v.reshape(Q * cells // LANES, LANES) for v in (populations, cotangent))
    w_mid = w_mid[0]
    pieces = piece_rows(blocks, slabs, hid)
    rows, most = 2 * sum(pieces), max(pieces)
    small, last = part_size(pieces[0], blocks, hid), part_size(pieces[-1], blocks // 2 * (slabs if DIRECT else 2), hid)
    pieces = len(pieces)
    volume = pltpu.VMEM((ROWS, LANES), F32)
    thin = pltpu.VMEM((R, cells), BF16)
    deep = pltpu.VMEM((hid, cells), BF16)
    slots = 2 * REACH + 3
    final, grad_pops, total = pl.pallas_call(
        functools.partial(step_kernel, blocks, slabs),
        out_shape=(shape(pops.shape), shape(pops.shape), shape((rows, hid))),
        in_specs=[SMEM_SPEC] * 3 + [pl.BlockSpec(memory_space=pltpu.HBM)] * 5,
        out_specs=tuple(vmem(3)),
        scratch_shapes=[
            pltpu.VMEM((rows, hid), F32),
            pltpu.VMEM((pieces, most, hid), F32),
            pltpu.VMEM((pieces, most, hid), F32),
            pltpu.VMEM((BIG, blocks - 1, *small), F32),
            pltpu.VMEM((blocks // 2 * (slabs if DIRECT else 2) - 1, *last), F32),
            pltpu.VMEM((pieces, *small), F32),
            pltpu.VMEM((pieces, max(slabs // 2 - 1, 1), *small), F32),
            pltpu.SemaphoreType.DMA((2, pieces, blocks * slabs + slabs // 2 + 1)),
        ] + [volume] * 4 + [thin] * 4 + [deep] * 6 + [pltpu.VMEM((hid, cells), F32)] + [
            *[pltpu.VMEM((3, SHEET_ROWS, LANES), F32)] * 4,
            *[pltpu.VMEM((slots, SHEET_ROWS, LANES), F32)] * 4,
            pltpu.VMEM((3, SHEET_ROWS, LANES), F32),
            pltpu.VMEM((4 * HALVES * 8, LANES), F32),
            pltpu.VMEM((16 * BLOCK, LANES), F32),
            pltpu.VMEM((10, A, A), BF16),
            pltpu.VMEM((hid, R), BF16),
            pltpu.VMEM((R, hid), BF16),
            pltpu.VMEM((R, hid), BF16),
            pltpu.VMEM((hid, R), BF16),
            pltpu.VMEM((hid, hid), BF16),
            pltpu.VMEM((R, hid), F32),
            pltpu.VMEM(pops.shape, F32),
            pltpu.VMEM(cot.shape, F32),
            pltpu.VMEM((Q, hid), BF16),
            pltpu.VMEM((hid, hid), BF16),
            pltpu.VMEM((Q, hid), BF16),
            pltpu.SemaphoreType.DMA((5,)),
            pltpu.SemaphoreType.DMA((4, 2, slots)),
        ],
        compiler_params=pltpu.CompilerParams(vmem_limit_bytes=LIMIT, collective_id=0, has_side_effects=True),
        name="step",
    )(*[
        pltpu.with_memory_space_constraint(v, pltpu.HBM)
        for v in (face_source.T, face_level, face_quadrant, pops, cot, w_in.T, w_mid, w_out)
    ])
    final, grad_pops, grad_mid, grad_in, grad_out = pl.pallas_call(
        leave_kernel,
        out_shape=(
            shape(pops.shape), shape(pops.shape), shape((hid, hid)), shape((Q, hid)), shape((Q, hid)),
        ),
        in_specs=vmem(3),
        out_specs=tuple([pl.BlockSpec(memory_space=pl.ANY)] * 5),
        scratch_shapes=[pltpu.VMEM((Q, hid), F32), pltpu.VMEM((Q, hid), F32), pltpu.SemaphoreType.DMA((5,))],
        compiler_params=pltpu.CompilerParams(vmem_limit_bytes=4 * 1024 * 1024),
        name="leave",
    )(final, grad_pops, total)
    return (
        final.reshape(populations.shape),
        grad_pops.reshape(populations.shape),
        grad_in.T,
        grad_mid[None],
        grad_out,
    )


def solution(mesh):
    spread = P(None, "slab", "blocks", None)
    in_specs = (spread, P(), P(), P(), spread, P(), P("slab", "blocks", None), P("slab", "blocks", None))
    out_specs = (spread, spread, P(), P(), P())
    body = functools.partial(shards, mesh.shape["blocks"], mesh.shape["slab"])
    return jax.shard_map(body, mesh=mesh, in_specs=in_specs, out_specs=out_specs, check_vma=False)
```
